768 devices in a mesh: dom: 192 (over y, z, core), depth: 4 (over x).
Axes of the slice: x: 4, y: 8, z: 12, core: 2. Of those that a mesh axis runs over, the one named last changes fastest.
Arguments:
- adjoint_now: float32 [3, 768, 68, 128], P(None, 'dom', 'depth'), may hold values from -6 to 6
- adjoint_next: float32 [3, 768, 68, 128], P(None, 'dom', 'depth'), may hold values from -6 to 6
- lame_first: float32 [192, 16, 32], P('dom', 'depth'), may hold values from 1 to 3
- shear_modulus: float32 [192, 16, 32], P('dom', 'depth'), may hold values from 1 to 3
- density: float32 [768, 68, 128], P('dom', 'depth'), may hold values from 1 to 3
- branch_flags: int32 [4, 4, 768, 128], P(None, 'depth', 'dom'), may hold values from 0 to 2
- weak_slope: float32 [4, 768, 128], P('depth', 'dom'), may hold values from 0.1 to 0.5
- normal_stress: float32 [4, 768, 128], P('depth', 'dom'), may hold values from 1 to 10
- patch_owner: int32 [4, 768], P('depth', 'dom'), may hold values from 0 to 383, as said below
Outputs:
- earlier_state: float32 [3, 768, 68, 128], P(None, 'dom', 'depth')
- later_state: float32 [3, 768, 68, 128], P(None, 'dom', 'depth')
- patch_gradient: float32 [4, 384, 128], P('depth', 'dom')
The draws below stay inside these ranges and needn't reach their ends.
Inputs may be any that keep to these rules, and one draw needn't show every extreme that they name: `patch_owner`: patch p is owned by dom index p // 2; a column held by dom index d belongs to a patch whose owner is at most 2 indices of dom from d.
All inputs are finite; a program needn't handle non-finite values.
Results may differ from the reference program's by a relative error of at most 0.0001.
Values sent between devices are 32-bit elements; how exact they have to be, the bound alone decides.
A program may use at most 32 MiB of HBM per device.

```python
import math
import jax
import jax.numpy as jnp
import numpy as np
from jax import lax

EX = 1
EY = 4
EZ = 32
STEPS = 4
PATCH_DEV = 2
REACH = 2
XE = 192
XG = 768
YE = 16
YG = 68
NZN = 128
N_DOM = 192
N_DEPTH = 4


def draw_patch_owner(key, part):
    columns = jnp.arange(4 * EX * N_DOM, dtype=jnp.int32)
    holder = columns // (4 * EX)
    first_key, second_key = jax.random.split(jax.random.fold_in(key, 11))
    offset = jax.random.randint(first_key, (N_DEPTH, 4 * EX * N_DOM), -REACH, REACH + 1)
    within = jax.random.randint(second_key, (N_DEPTH, 4 * EX * N_DOM), 0, PATCH_DEV)
    owner_index = jnp.clip(holder[None, :] + offset, 0, N_DOM - 1)
    numbers = owner_index * PATCH_DEV + within
    numbers = jnp.where(columns[None, :] == 4 * EX * N_DOM - 1, PATCH_DEV * N_DOM - 1, numbers)
    numbers = jnp.where(columns[None, :] == 0, 0, numbers)
    return numbers.astype(jnp.int32)


def plant(values, stream_key, smallest, high):
    longest = values.shape.index(max(values.shape))
    spots = []
    for shift in (0, 1):
        where = [jax.random.randint(jax.random.fold_in(stream_key, axis), (), 0, length) for axis, length in enumerate(values.shape)]
        where[longest] = (where[longest] + shift) % values.shape[longest]
        spots.append(tuple(where))
    return values.at[spots[0]].set(smallest).at[spots[1]].set(high)


def shard_levels(key, shape, shards, smallest, high):
    factor_of = 1.0
    for axis_at, blocks in shards:
        heights = jax.random.uniform(jax.random.fold_in(jax.random.fold_in(key, 6), axis_at), (blocks,), jnp.float32, smallest / len(shards), high / len(shards))
        factor_of = factor_of * jnp.repeat(jnp.exp(heights), shape[axis_at] // blocks).reshape((-1,) + (1,) * (len(shape) - 1 - axis_at))
    return factor_of


def noise(rng, extent, deviation, bound, cuts=(), kind=jnp.bfloat16):
    result = deviation * jax.random.normal(rng, extent, jnp.float32)
    if cuts:
        result = result * shard_levels(rng, extent, cuts, -0.22, 0.18)
    return jnp.clip(result, -bound, bound).astype(kind)


def setup_inputs(seed: int = 0) -> dict:
    splits = jax.random.split(jax.random.key(seed), 10)
    return {
        "adjoint_now": noise(splits[0], (3, XG, YG, NZN), 1.0, 6.0, ((1, 192), (2, 4)), jnp.float32),
        "adjoint_next": noise(splits[1], (3, XG, YG, NZN), 1.0, 6.0, ((1, 192), (2, 4)), jnp.float32),
        "lame_first": jnp.clip(jnp.exp(math.log(3.0) - 1.0986123 * jax.random.uniform(splits[2], (XE, YE, EZ), jnp.float32) ** shard_levels(splits[2], (XE, YE, EZ), ((0, 192), (1, 4)), -0.2, 0.2)), 1.0, 3.0),
        "shear_modulus": jnp.clip(jnp.exp(math.log(3.0) - 1.0986123 * jax.random.uniform(splits[3], (XE, YE, EZ), jnp.float32) ** shard_levels(splits[3], (XE, YE, EZ), ((0, 192), (1, 4)), -0.2, 0.2)), 1.0, 3.0),
        "density": jnp.clip(jnp.exp(math.log(3.0) - 1.0986123 * jax.random.uniform(splits[4], (XG, YG, NZN), jnp.float32) ** shard_levels(splits[4], (XG, YG, NZN), ((0, 192), (1, 4)), -0.2, 0.2)), 1.0, 3.0),
        "branch_flags": plant(jax.random.randint(splits[5], (STEPS, N_DEPTH, XG, NZN), 0, 3), jax.random.fold_in(splits[5], 1), 0, 2).astype(jnp.int32),
        "weak_slope": jnp.clip(jnp.exp(math.log(0.5) - 1.609438 * jax.random.uniform(splits[6], (N_DEPTH, XG, NZN), jnp.float32) ** shard_levels(splits[6], (N_DEPTH, XG, NZN), ((0, 4), (1, 192)), -0.2, 0.2)), 0.1, 0.5),
        "normal_stress": jnp.clip(jnp.exp(math.log(10.0) - 2.3025851 * jax.random.uniform(splits[7], (N_DEPTH, XG, NZN), jnp.float32) ** shard_levels(splits[7], (N_DEPTH, XG, NZN), ((0, 4), (1, 192)), -0.2, 0.2)), 1.0, 10.0),
        "patch_owner": draw_patch_owner(jax.random.fold_in(splits[9], 71), 0),
    }


time_step = 0.01
lock_stiffness = 0.5
highest = lax.Precision.HIGHEST

def basis_tables():
    points = [-1.0, -math.sqrt(3.0 / 7.0), 0.0, math.sqrt(3.0 / 7.0), 1.0]
    quad_weights = np.array([0.1, 49.0 / 90.0, 32.0 / 45.0, 49.0 / 90.0, 0.1])
    products = []
    for first in range(5):
        value = 1.0
        for other in range(5):
            if other != first:
                value = value * (points[first] - points[other])
        products.append(value)
    derivative = np.zeros((5, 5))
    for row in range(5):
        for column in range(5):
            if row == column:
                total = 0.0
                for other in range(5):
                    if other != row:
                        total = total + 1.0 / (points[row] - points[other])
                derivative[row, column] = total
            else:
                derivative[row, column] = products[row] / products[column] / (points[row] - points[column])
    return (quad_weights, derivative)

def element_maps(elements):
    quad_weights, derivative = basis_tables()
    expand = np.zeros((5 * elements, 4 * elements + 1))
    slopes = np.zeros((5 * elements, 4 * elements + 1))
    for element in range(elements):
        for corner in range(5):
            expand[5 * element + corner, 4 * element + corner] = 1.0
            slopes[5 * element + corner, 4 * element:4 * element + 5] = 2.0 * derivative[corner]
    return (expand, slopes, np.tile(quad_weights, elements))

def stiffness(displaced, lame_block, shear_block):
    x_elems, y_elems, z_elems = lame_block.shape
    maps_x = element_maps(x_elems)
    maps_y = element_maps(y_elems)
    maps_z = element_maps(z_elems)
    x_expand = jnp.asarray(maps_x[0], dtype=jnp.float32)
    x_slopes = jnp.asarray(maps_x[1], dtype=jnp.float32)
    y_expand = jnp.asarray(maps_y[0], dtype=jnp.float32)
    y_slopes = jnp.asarray(maps_y[1], dtype=jnp.float32)
    z_expand = jnp.asarray(maps_z[0], dtype=jnp.float32)
    z_slopes = jnp.asarray(maps_z[1], dtype=jnp.float32)
    weight_x = jnp.asarray(maps_x[2], dtype=jnp.float32)
    weight_y = jnp.asarray(maps_y[2], dtype=jnp.float32)
    weight_z = jnp.asarray(maps_z[2], dtype=jnp.float32)
    along_z = jnp.einsum('cxyz,qz->cxyq', displaced, z_expand, precision=highest)
    slope_z = jnp.einsum('cxyz,qz->cxyq', displaced, z_slopes, precision=highest)
    plain_yz = jnp.einsum('cxyq,py->cxpq', along_z, y_expand, precision=highest)
    slope_y = jnp.einsum('cxyq,py->cxpq', along_z, y_slopes, precision=highest)
    slope_zy = jnp.einsum('cxyq,py->cxpq', slope_z, y_expand, precision=highest)
    grad_x = jnp.einsum('cxpq,rx->crpq', plain_yz, x_slopes, precision=highest)
    grad_y = jnp.einsum('cxpq,rx->crpq', slope_y, x_expand, precision=highest)
    grad_z = jnp.einsum('cxpq,rx->crpq', slope_zy, x_expand, precision=highest)
    weight_q = weight_x[:, None, None] * weight_y[None, :, None] * weight_z[None, None, :] / 8.0
    lame_q = jnp.repeat(jnp.repeat(jnp.repeat(lame_block, 5, axis=0), 5, axis=1), 5, axis=2)
    shear_q = jnp.repeat(jnp.repeat(jnp.repeat(shear_block, 5, axis=0), 5, axis=1), 5, axis=2)
    divergence = grad_x[0] + grad_y[1] + grad_z[2]
    normal_part = lame_q * divergence
    stress_xx = normal_part + 2.0 * shear_q * grad_x[0]
    stress_yy = normal_part + 2.0 * shear_q * grad_y[1]
    stress_zz = normal_part + 2.0 * shear_q * grad_z[2]
    stress_xy = shear_q * (grad_x[1] + grad_y[0])
    stress_xz = shear_q * (grad_x[2] + grad_z[0])
    stress_yz = shear_q * (grad_y[2] + grad_z[1])
    flux_x = weight_q * jnp.stack([stress_xx, stress_xy, stress_xz])
    flux_y = weight_q * jnp.stack([stress_xy, stress_yy, stress_yz])
    flux_z = weight_q * jnp.stack([stress_xz, stress_yz, stress_zz])
    back_x = jnp.einsum('crpq,rx->cxpq', flux_x, x_slopes, precision=highest)
    back_y = jnp.einsum('crpq,rx->cxpq', flux_y, x_expand, precision=highest)
    back_z = jnp.einsum('crpq,rx->cxpq', flux_z, x_expand, precision=highest)
    partial_a = jnp.einsum('cxpq,py->cxyq', back_x, y_expand, precision=highest) + jnp.einsum('cxpq,py->cxyq', back_y, y_slopes, precision=highest)
    partial_b = jnp.einsum('cxpq,py->cxyq', back_z, y_expand, precision=highest)
    return jnp.einsum('cxyq,qz->cxyz', partial_a, z_expand, precision=highest) + jnp.einsum('cxyq,qz->cxyz', partial_b, z_slopes, precision=highest)

def clamped_stiffness(displaced, lame_block, shear_block):
    padded = jnp.concatenate([displaced, jnp.zeros_like(displaced[..., :1])], axis=-1)
    return stiffness(padded, lame_block, shear_block)[..., :displaced.shape[-1]]

def fault_force(tangent, slip_vector):
    return jnp.stack([tangent * slip_vector[0], lock_stiffness * slip_vector[1], tangent * slip_vector[2]])

def volume_forces(field_now, lame_first, shear_modulus):
    owned_nodes = 4 * EX
    slab_nodes = 4 * EY + 1
    blocked = field_now.reshape(3, N_DOM, owned_nodes, N_DEPTH, slab_nodes, 4 * EZ)
    next_planes = jnp.concatenate([blocked[:, 1:, :1], jnp.zeros_like(blocked[:, :1, :1])], axis=1)
    extended = jnp.concatenate([blocked, next_planes], axis=2)
    extended = jnp.transpose(extended, (1, 3, 0, 2, 4, 5))
    lame_blocks = jnp.transpose(lame_first.reshape(N_DOM, EX, N_DEPTH, EY, EZ), (0, 2, 1, 3, 4))
    shear_blocks = jnp.transpose(shear_modulus.reshape(N_DOM, EX, N_DEPTH, EY, EZ), (0, 2, 1, 3, 4))

    def per_block(entries):
        return jax.vmap(clamped_stiffness)(entries[0], entries[1], entries[2])
    element_forces = lax.map(per_block, (extended, lame_blocks, shear_blocks))
    end_planes = element_forces[:, :, :, owned_nodes]
    carried = jnp.concatenate([jnp.zeros_like(end_planes[:1]), end_planes[:-1]], axis=0)
    owned_part = element_forces[:, :, :, :owned_nodes].at[:, :, :, 0].add(carried)
    return jnp.transpose(owned_part, (2, 0, 3, 1, 4, 5)).reshape(field_now.shape)

def reference(adjoint_now, adjoint_next, lame_first, shear_modulus, density, branch_flags, weak_slope, normal_stress, patch_owner):
    slab_nodes = 4 * EY + 1
    depth_nodes = 4 * EZ
    strike_nodes = 4 * EX * N_DOM
    maps_x = element_maps(EX * N_DOM)
    maps_y = element_maps(EY)
    maps_z = element_maps(EZ)
    mass_x = jnp.asarray((maps_x[0].T @ maps_x[2])[:strike_nodes], dtype=jnp.float32)
    mass_y = jnp.asarray(np.tile(maps_y[0].T @ maps_y[2], N_DEPTH), dtype=jnp.float32)
    mass_z = jnp.asarray((maps_z[0].T @ maps_z[2])[:depth_nodes], dtype=jnp.float32)
    nodal_mass = density * mass_x[:, None, None] * mass_y[None, :, None] * mass_z[None, None, :] / 8.0
    tangent = jnp.where(branch_flags == 0, lock_stiffness, jnp.where(branch_flags == 1, -weak_slope[None], 0.0))
    response = jnp.where(branch_flags == 1, 0.5, jnp.where(branch_flags == 2, 1.0, 0.0))
    current, following = (adjoint_now, adjoint_next)
    gradient = jnp.zeros((N_DEPTH, strike_nodes, depth_nodes), jnp.float32)
    for section_index in range(STEPS):
        forces = volume_forces(current, lame_first, shear_modulus)
        slab_view = current.reshape(3, strike_nodes, N_DEPTH, slab_nodes, depth_nodes)
        minus_plane = jnp.transpose(slab_view[:, :, :, -1], (0, 2, 1, 3))
        lower_plane = jnp.transpose(slab_view[:, :, :, 0], (0, 2, 1, 3))
        plus_plane = jnp.roll(lower_plane, -1, axis=1)
        slip_vector = plus_plane - minus_plane
        pulled = fault_force(tangent[section_index], slip_vector)
        gradient = gradient + normal_stress * response[section_index] * slip_vector[0]
        from_below = jnp.roll(pulled, 1, axis=1)
        net_force = (-forces).reshape(3, strike_nodes, N_DEPTH, slab_nodes, depth_nodes)
        net_force = net_force.at[:, :, :, -1].add(jnp.transpose(pulled, (0, 2, 1, 3)))
        net_force = net_force.at[:, :, :, 0].add(-jnp.transpose(from_below, (0, 2, 1, 3)))
        net_force = net_force.reshape(current.shape)
        updated = 2.0 * current - following + time_step * time_step * (net_force / nodal_mass)
        following, current = (current, updated)

    def strand_sums(strand_gradient, strand_owner):
        return jax.ops.segment_sum(strand_gradient, strand_owner, num_segments=PATCH_DEV * N_DOM)
    patch_sums = jax.vmap(strand_sums)(gradient, patch_owner)
    return (current, following, patch_sums)
```

```python
import functools
import math

import jax
import jax.numpy as jnp
import numpy as np
from jax import lax
from jax.experimental import pallas as pl
from jax.experimental.pallas import tpu as pltpu
from jax.sharding import PartitionSpec as P


MESH = pl.DeviceIdType.MESH
STEPS = 4
ROWS = 80
DT2 = 0.01 * 0.01
LOCK = 0.5
W5 = [0.1, 49.0 / 90.0, 32.0 / 45.0, 49.0 / 90.0, 0.1]
OFFSETS = (-2, -1, 1, 2)
f32 = jnp.float32


def slopes5():
    pts = [-1.0, -math.sqrt(3.0 / 7.0), 0.0, math.sqrt(3.0 / 7.0), 1.0]
    prod = [np.prod([pts[a] - pts[b] for b in range(5) if b != a]) for a in range(5)]
    d = np.zeros((5, 5))
    for a in range(5):
        for b in range(5):
            if a == b:
                d[a, b] = sum(1.0 / (pts[a] - pts[o]) for o in range(5) if o != a)
            else:
                d[a, b] = prod[a] / prod[b] / (pts[a] - pts[b])
    d[2, 2] = 0.0
    return 2.0 * d


D5 = slopes5()


def apply5(m, v):
    e0, e1, o0, o1 = v[0] + v[4], v[1] + v[3], v[0] - v[4], v[1] - v[3]
    out = [None] * 5
    for q in (0, 1):
        a = (
            float((m[q, 0] + m[q, 4]) / 2) * e0
            + float((m[q, 1] + m[q, 3]) / 2) * e1
            + float(m[q, 2]) * v[2]
        )
        b = float((m[q, 0] - m[q, 4]) / 2) * o0 + float((m[q, 1] - m[q, 3]) / 2) * o1
        out[q] = b + a
        out[4 - q] = b - a
    out[2] = float((m[2, 0] - m[2, 4]) / 2) * o0 + float((m[2, 1] - m[2, 3]) / 2) * o1
    return out


def wkey(a, b):
    a, b = min(a, 4 - a), min(b, 4 - b)
    a, b = min(a, b), max(a, b)
    return {(0, 0): 0, (0, 1): 1, (0, 2): 2, (1, 1): 3, (1, 2): 4, (2, 2): 5}[(a, b)]


WPAIR = [(0, 0), (0, 1), (0, 2), (1, 1), (1, 2), (2, 2)]


def rblk(c, yl, zl):
    return (c * 5 + yl) * 5 + zl


def kernel(
    nd,
    ndp,
    now,
    nxt,
    lam,
    mu,
    dens,
    flags,
    slope,
    ns,
    owner,
    out_cur,
    out_fol,
    out_patch,
    nowv,
    nxtv,
    densv,
    lamv,
    muv,
    flagv,
    slopev,
    nsv,
    ownv,
    gnow,
    gnxt,
    gdens,
    gflag,
    gslope,
    stage,
    S,
    F,
    GY,
    FX,
    FY,
    IM,
    IMP,
    CONST,
    TH,
    grad,
    send_dom,
    recv_dom,
    send_dep,
    recv_dep,
    psend,
    precv,
    outv,
    patchv,
    lsem,
    isend,
    irecv,
    dsend,
    drecv,
    fsend,
    frecv,
    pss,
    prs,
    osem,
):
    me = lax.axis_index("dom")
    my = lax.axis_index("depth")
    up = lax.rem(my + 1, ndp)
    dn = lax.rem(my + ndp - 1, ndp)
    has_l = me > 0
    has_r = me < nd - 1

    locals_ = [
        pltpu.make_async_copy(a, b, lsem.at[i])
        for i, (a, b) in enumerate(
            [
                (now, nowv),
                (nxt, nxtv),
                (dens, densv),
                (lam, lamv),
                (mu, muv),
                (flags, flagv),
                (slope, slopev),
                (ns, nsv),
                (owner, ownv),
            ]
        )
    ]
    for cp in locals_:
        cp.start()

    barrier = pltpu.get_barrier_semaphore()
    count = 2
    pl.semaphore_signal(barrier, inc=1, device_id=(me, up), device_id_type=MESH)
    pl.semaphore_signal(barrier, inc=1, device_id=(me, dn), device_id_type=MESH)
    for off, row in ((-1, my), (1, my), (-2, my), (2, my), (-1, up), (1, dn)):
        ok = jnp.logical_and(me + off >= 0, me + off < nd)
        count = count + ok.astype(jnp.int32)

        @pl.when(ok)
        def _(off=off, row=row):
            pl.semaphore_signal(
                barrier, inc=1, device_id=(me + off, row), device_id_type=MESH
            )

    pl.semaphore_wait(barrier, count)

    def remote(i, src, dst, to):
        return pltpu.make_async_remote_copy(
            src_ref=src,
            dst_ref=dst,
            send_sem=isend.at[i],
            recv_sem=irecv.at[i],
            device_id=to,
            device_id_type=MESH,
        )

    to_left = [
        remote(0, now.at[:, 0], gnow, (me - 1, my)),
        remote(1, nxt.at[:, 0], gnxt, (me - 1, my)),
        remote(2, dens.at[0], gdens, (me - 1, my)),
        remote(3, flags, gflag.at[0], (me - 1, my)),
        remote(4, slope, gslope.at[0], (me - 1, my)),
        remote(5, flags, gflag.at[1], (me - 1, up)),
        remote(6, slope, gslope.at[1], (me - 1, up)),
    ]
    to_up = [
        remote(7, flags, gflag.at[2], (me, up)),
        remote(8, slope, gslope.at[2], (me, up)),
    ]

    @pl.when(has_l)
    def _():
        for cp in to_left:
            cp.start()

    for cp in to_up:
        cp.start()

    lane = lax.broadcasted_iota(jnp.int32, (8, 128), 1)
    sub = lax.broadcasted_iota(jnp.int32, (8, 128), 0)
    blk = lane // 32
    ez = lane % 32
    to_packed = 4 * ez + blk
    to_natural = (lane % 4) * 32 + lane // 4
    b0, b1, b2, b3 = blk == 0, blk == 1, blk == 2, blk == 3

    def permute(x, idx):
        return jnp.take_along_axis(x, idx, axis=1)

    def roll(x, shift):
        shift = shift % 128
        return x if shift == 0 else pltpu.roll(x, shift, 1)

    def by_sub(vals):
        v = jnp.full((8, 128), 0.0, f32)
        for i, x in enumerate(vals):
            if x != 0.0:
                v = jnp.where(sub == i, float(x), v)
        return v

    for k in range(5):
        CONST[k] = by_sub(D5[:, k])
        CONST[5 + k] = by_sub(D5[k, :])

    stage[...] = jnp.zeros(stage.shape, f32)
    for i in range(75, ROWS):
        F[pl.ds(8 * i, 8), :] = jnp.zeros((8, 128), f32)
        S[0, pl.ds(8 * i, 8), :] = jnp.zeros((8, 128), f32)
        S[1, pl.ds(8 * i, 8), :] = jnp.zeros((8, 128), f32)

    def pick(r0, r1, r2, r3):
        return jnp.where(b0, r0, jnp.where(b1, r1, jnp.where(b2, r2, r3)))

    def to_elements(c, put, bottom):
        packed = [
            permute(stage[pl.ds(c * 192 + y, 8, stride=24), :], to_packed)
            for y in range(17)
        ]
        rolled = [[roll(v, 32 * s) for s in range(4)] for v in packed]
        for yl in range(5):
            for zl in range(4):
                v = pick(*[rolled[4 * e + yl][(e - zl) % 4] for e in range(4)])
                put(yl, zl, v)
                if zl == 0:
                    first = v
            put(yl, 4, jnp.where(ez == 31, bottom, roll(first, -1)))

    for cp in locals_:
        cp.wait()

    @pl.when(has_r)
    def _():
        for cp in to_left:
            cp.wait_recv()

    for cp in to_up:
        cp.wait_recv()

    def fill(own, ghost, slot):
        for c in range(3):
            for x in range(4):
                stage[pl.ds((c * 8 + x) * 24, 17), :] = own[c, x]
            stage[pl.ds((c * 8 + 4) * 24, 17), :] = jnp.where(has_r, ghost[c], 0.0)
        for c in range(3):

            def put(yl, zl, v, c=c):
                S[slot, pl.ds(8 * rblk(c, yl, zl), 8), :] = v

            to_elements(c, put, 0.0)

    fill(nowv, gnow, 0)
    fill(nxtv, gnxt, 1)

    for x in range(4):
        stage[pl.ds(x * 24, 17), :] = densv[x]
    stage[pl.ds(4 * 24, 17), :] = jnp.where(has_r, gdens[...], 1.0)
    wx = by_sub([0.2, W5[1], W5[2], W5[3], 0.2])
    wx = jnp.where(sub == 0, jnp.where(has_l, 0.2, 0.1), wx)
    live_x = jnp.logical_or(sub < 4, jnp.logical_and(sub == 4, has_r))

    def put_mass(yl, zl, v):
        if yl in (1, 2, 3):
            wy = W5[yl]
        else:
            wy = jnp.where(b0 if yl == 0 else b3, 0.1, 0.2)
        if zl in (1, 2, 3):
            wz = W5[zl]
        elif zl == 0:
            wz = jnp.where(ez == 0, 0.1, 0.2)
        else:
            wz = 0.2
        mass = v * wx * wy * wz
        live = jnp.logical_and(live_x, ez < 31) if zl == 4 else live_x
        IM[pl.ds(8 * (yl * 5 + zl), 8), :] = jnp.where(
            live, (8.0 * DT2) / jnp.where(live, mass, 1.0), 0.0
        )

    to_elements(0, put_mass, 1.0)
    for c in range(3):
        for i in range(25):
            IMP[0, pl.ds(25 * c + i, 1), :] = IM[pl.ds(8 * i, 1), :]
            IMP[1, pl.ds(25 * c + i, 1), :] = IM[pl.ds(8 * i + 4, 1), :]
    for i in range(75, ROWS):
        IMP[0, pl.ds(i, 1), :] = jnp.zeros((1, 128), f32)
        IMP[1, pl.ds(i, 1), :] = jnp.zeros((1, 128), f32)

    def wide(ref):
        z = jnp.zeros((1, 96), f32)
        out = jnp.zeros((8, 128), f32)
        for e in range(4):
            row = jnp.concatenate([ref[0, pl.ds(e, 1), :], z], axis=1)
            row = jnp.broadcast_to(row, (8, 128))
            out = jnp.where(blk == e, roll(row, 32 * e), out)
        return out

    wq = by_sub([w / 8.0 for w in W5])
    lam_x = wide(lamv) * wq
    mu_x = wide(muv) * wq
    for i, (a, b) in enumerate(WPAIR):
        w = float(W5[a] * W5[b])
        CONST[10 + i] = lam_x * w
        CONST[16 + i] = mu_x * w

    def planes(own, ghost):
        top = jnp.concatenate([own, jnp.zeros((4, 128), own.dtype)], axis=0)
        low = jnp.concatenate([ghost, ghost], axis=0)
        return jnp.where(sub == 4, low, top)

    def spread(ghost):
        return jnp.broadcast_to(ghost[0:1], (4, 128))

    live5 = live_x

    for i in range(STEPS):
        own_f = planes(flagv[i, 0], spread(gflag[0, i, 0]))
        low_f = planes(gflag[2, i, 0], spread(gflag[1, i, 0]))
        own_s = planes(slopev[0], spread(gslope[0, 0]))
        low_s = planes(gslope[2, 0], spread(gslope[1, 0]))
        for j, (fl, sl) in enumerate(((own_f, own_s), (low_f, low_s))):
            t = jnp.where(fl == 0, LOCK, jnp.where(fl == 1, -sl, 0.0))
            t = jnp.where(live5, t, 0.0)
            TH[j, i] = permute(t, to_packed)
        h = jnp.where(own_f == 1, 0.5, jnp.where(own_f == 2, 1.0, 0.0))
        stress = jnp.concatenate([nsv[0], jnp.zeros((4, 128), f32)], axis=0)
        TH[2, i] = permute(jnp.where(sub < 4, h * stress, 0.0), to_packed)

    grad[...] = jnp.zeros((8, 128), f32)

    def dom_copy(side, step):
        to = me - 1 if side == 0 else me + 1
        return pltpu.make_async_remote_copy(
            src_ref=send_dom.at[side, step],
            dst_ref=recv_dom.at[side, step],
            send_sem=dsend.at[side, step],
            recv_sem=drecv.at[side, step],
            device_id=(to, my),
            device_id_type=MESH,
        )

    def dep_copy(side, step):
        to = dn if side == 0 else up
        return pltpu.make_async_remote_copy(
            src_ref=send_dep.at[side, step],
            dst_ref=recv_dep.at[side, step],
            send_sem=fsend.at[side, step],
            recv_sem=frecv.at[side, step],
            device_id=(me, to),
            device_id_type=MESH,
        )

    def patch_copy(i):
        return pltpu.make_async_remote_copy(
            src_ref=psend.at[i],
            dst_ref=precv.at[i],
            send_sem=pss.at[i],
            recv_sem=prs.at[i],
            device_id=(me + OFFSETS[i], my),
            device_id_type=MESH,
        )

    def inside(v):
        return jnp.logical_and(v >= 0, v < nd)

    def step_body(step, carry):
        cur = lax.rem(step, 2)
        new = 1 - cur

        def u(c, yl, zl):
            return S[cur, pl.ds(8 * rblk(c, yl, zl), 8), :]

        for c in range(3):
            low = [roll(u(c, 0, z), 32 * z) for z in range(4)]
            high = [roll(u(c, 4, z), 32 * (z - 3)) for z in range(4)]
            send_dep[0, step, c] = pick(*low)
            send_dep[1, step, c] = pick(*high)
        dep_copy(0, step).start()
        dep_copy(1, step).start()

        for c in range(3):
            for zl in range(5):
                g = apply5(D5, [u(c, yl, zl) for yl in range(5)])
                for yl in range(5):
                    GY[pl.ds(8 * rblk(c, yl, zl), 8), :] = g[yl]
        for yl in range(5):
            gz = [apply5(D5, [u(c, yl, zl) for zl in range(5)]) for c in range(3)]
            fz = [[None] * 5 for _ in range(3)]
            for zl in range(5):
                gx, gy = [], []
                for c in range(3):
                    r = 8 * rblk(c, yl, zl)
                    acc = None
                    for k in range(5):
                        row = jnp.broadcast_to(S[cur, pl.ds(r + k, 1), :], (8, 128))
                        t = row * CONST[k]
                        acc = t if acc is None else acc + t
                    gx.append(acc)
                    gy.append(GY[pl.ds(r, 8), :])
                key = wkey(yl, zl)
                lw, mw = CONST[10 + key], CONST[16 + key]
                m2 = mw + mw
                common = lw * (gx[0] + gy[1] + gz[2][zl])
                sxx = common + m2 * gx[0]
                syy = common + m2 * gy[1]
                szz = common + m2 * gz[2][zl]
                sxy = mw * (gx[1] + gy[0])
                sxz = mw * (gx[2] + gz[0][zl])
                syz = mw * (gy[2] + gz[1][zl])
                for c, (vx, vy, vz) in enumerate(
                    ((sxx, sxy, sxz), (sxy, syy, syz), (sxz, syz, szz))
                ):
                    r = 8 * rblk(c, yl, zl)
                    FX[pl.ds(r, 8), :] = vx
                    FY[pl.ds(r, 8), :] = vy
                    fz[c][zl] = vz
            for c in range(3):
                back = apply5(D5.T, fz[c])
                for zl in range(5):
                    F[pl.ds(8 * rblk(c, yl, zl), 8), :] = back[zl]
        for c in range(3):
            for zl in range(5):
                rs = [8 * rblk(c, yl, zl) for yl in range(5)]
                back = apply5(D5.T, [FY[pl.ds(r, 8), :] for r in rs])
                for yl, r in enumerate(rs):
                    acc = back[yl] + F[pl.ds(r, 8), :]
                    for q in range(5):
                        row = jnp.broadcast_to(FX[pl.ds(r + q, 1), :], (8, 128))
                        acc = acc + row * CONST[5 + q]
                    F[pl.ds(r, 8), :] = acc

        for c in range(3):
            for yl in range(5):
                ra, rb = 8 * rblk(c, yl, 0), 8 * rblk(c, yl, 4)
                fa, fb = F[pl.ds(ra, 8), :], F[pl.ds(rb, 8), :]
                F[pl.ds(ra, 8), :] = fa + jnp.where(ez == 0, 0.0, roll(fb, 1))
                F[pl.ds(rb, 8), :] = fb + roll(fa, -1)
        for c in range(3):
            for zl in range(5):
                ra, rb = 8 * rblk(c, 0, zl), 8 * rblk(c, 4, zl)
                fa, fb = F[pl.ds(ra, 8), :], F[pl.ds(rb, 8), :]
                F[pl.ds(ra, 8), :] = fa + jnp.where(b0, 0.0, roll(fb, 32))
                F[pl.ds(rb, 8), :] = fb + jnp.where(b3, 0.0, roll(fa, -32))

        for g in range(ROWS // 8):
            send_dom[0, step, pl.ds(8 * g, 8), :] = F[pl.ds(64 * g, 8, stride=8), :]
            send_dom[1, step, pl.ds(8 * g, 8), :] = F[pl.ds(64 * g + 4, 8, stride=8), :]

        @pl.when(has_l)
        def _():
            dom_copy(0, step).start()

        @pl.when(has_r)
        def _():
            dom_copy(1, step).start()

        dep_copy(0, step).wait_recv()
        dep_copy(1, step).wait_recv()
        slip0 = None
        for c in range(3):
            slip_hi = recv_dep[0, step, c] - send_dep[1, step, c]
            slip_lo = send_dep[0, step, c] - recv_dep[1, step, c]
            if c == 0:
                slip0 = slip_hi
            t_hi = LOCK if c == 1 else TH[0, step]
            t_lo = LOCK if c == 1 else TH[1, step]
            hi = t_hi * slip_hi
            lo = t_lo * slip_lo
            for zl in range(5):
                sh = (96, 0) if zl < 4 else (95, -1)
                zb = zl if zl < 4 else 0
                rh, rl = 8 * rblk(c, 4, zl), 8 * rblk(c, 0, zl)
                F[pl.ds(rh, 8), :] = F[pl.ds(rh, 8), :] - jnp.where(
                    b3, roll(hi, sh[0] - 32 * zb), 0.0
                )
                F[pl.ds(rl, 8), :] = F[pl.ds(rl, 8), :] + jnp.where(
                    b0, roll(lo, sh[1] - 32 * zb), 0.0
                )
        grad[...] = grad[...] + TH[2, step] * slip0

        for yl in range(5):
            for zl in range(5):
                im = IM[pl.ds(8 * (yl * 5 + zl), 8), :]
                for c in range(3):
                    r = pl.ds(8 * rblk(c, yl, zl), 8)
                    now_u = S[cur, r, :]
                    S[new, r, :] = (now_u + now_u) - S[new, r, :] - im * F[r, :]

        def add_side(side, first):
            for g in range(ROWS // 8):
                r = pl.ds(64 * g + first, 8, stride=8)
                d = pl.ds(8 * g, 8)
                plane = 0 if first == 0 else 1
                S[new, r, :] = S[new, r, :] - IMP[plane, d, :] * recv_dom[side, step, d, :]

        @pl.when(has_l)
        def _():
            dom_copy(1, step).wait_recv()
            add_side(1, 0)

        @pl.when(has_r)
        def _():
            dom_copy(0, step).wait_recv()
            add_side(0, 4)

        return carry

    lax.fori_loop(0, STEPS, step_body, 0)

    total = permute(grad[...], to_natural)
    rows = [total[x : x + 1] for x in range(4)]

    def members(off, p):
        num = (me + off) * 2 + p
        acc = jnp.zeros((1, 128), f32)
        for x in range(4):
            acc = acc + jnp.where(ownv[0, x] == num, rows[x], 0.0)
        return acc

    for i, off in enumerate(OFFSETS):
        psend[i] = jnp.zeros((8, 128), f32)
        for p in range(2):
            psend[i, pl.ds(p, 1), :] = members(off, p)

        @pl.when(inside(me + off))
        def _(i=i):
            patch_copy(i).start()

    patchv[0, pl.ds(0, 1), :] = members(0, 0)
    patchv[0, pl.ds(1, 1), :] = members(0, 1)

    def from_elements(slot, which, out):
        for c in range(3):
            def e(yl, zl):
                return S[slot, pl.ds(8 * rblk(c, yl, zl), 8), :]

            for y in range(17):
                ey, yl = (y // 4, y % 4) if y < 16 else (3, 4)
                v = pick(*[roll(e(yl, zl), 32 * (zl - ey)) for zl in range(4)])
                stage[pl.ds(c * 192 + y, 8, stride=24), :] = permute(v, to_natural)
        for c in range(3):
            for x in range(4):
                outv[which, c, x] = stage[pl.ds((c * 8 + x) * 24, 17), :]
        cp = pltpu.make_async_copy(outv.at[which], out, osem.at[which])
        cp.start()
        return cp

    cps = [from_elements(STEPS % 2, 0, out_cur), from_elements(1 - STEPS % 2, 1, out_fol)]

    for i, off in enumerate(OFFSETS):

        @pl.when(inside(me - off))
        def _(i=i):
            patch_copy(i).wait_recv()
            patchv[0] = patchv[0] + precv[i, pl.ds(0, 2), :]

    cp = pltpu.make_async_copy(patchv, out_patch, osem.at[2])
    cp.start()
    cps.append(cp)

    @pl.when(has_l)
    def _():
        for cp in to_left:
            cp.wait_send()
        for s in range(STEPS):
            dom_copy(0, s).wait_send()

    @pl.when(has_r)
    def _():
        for s in range(STEPS):
            dom_copy(1, s).wait_send()

    for cp in to_up:
        cp.wait_send()
    for s in range(STEPS):
        dep_copy(0, s).wait_send()
        dep_copy(1, s).wait_send()
    for i, off in enumerate(OFFSETS):

        @pl.when(inside(me + off))
        def _(i=i):
            patch_copy(i).wait_send()

    for cp in cps:
        cp.wait()


def solution(mesh):
    nd, ndp = mesh.shape["dom"], mesh.shape["depth"]

    def on_device(now, nxt, lam, mu, dens, flags, slope, ns, owner):
        any_ = pl.BlockSpec(memory_space=pl.ANY)
        dma = pltpu.SemaphoreType.DMA
        vm = pltpu.VMEM
        i32 = jnp.int32
        return pl.pallas_call(
            functools.partial(kernel, nd, ndp),
            name="rupture",
            out_shape=(
                jax.ShapeDtypeStruct((3, 4, 17, 128), f32),
                jax.ShapeDtypeStruct((3, 4, 17, 128), f32),
                jax.ShapeDtypeStruct((1, 2, 128), f32),
            ),
            in_specs=[any_] * 9,
            out_specs=[any_] * 3,
            scratch_shapes=[
                vm((3, 4, 17, 128), f32),
                vm((3, 4, 17, 128), f32),
                vm((4, 17, 128), f32),
                vm((1, 4, 32), f32),
                vm((1, 4, 32), f32),
                vm((4, 1, 4, 128), i32),
                vm((1, 4, 128), f32),
                vm((1, 4, 128), f32),
                pltpu.SMEM((1, 4), i32),
                vm((3, 17, 128), f32),
                vm((3, 17, 128), f32),
                vm((17, 128), f32),
                vm((3, 4, 1, 4, 128), i32),
                vm((3, 1, 4, 128), f32),
                vm((3 * 8 * 24, 128), f32),
                vm((2, ROWS * 8, 128), f32),
                vm((ROWS * 8, 128), f32),
                vm((ROWS * 8, 128), f32),
                vm((ROWS * 8, 128), f32),
                vm((ROWS * 8, 128), f32),
                vm((25 * 8, 128), f32),
                vm((2, ROWS, 128), f32),
                vm((22, 8, 128), f32),
                vm((3, STEPS, 8, 128), f32),
                vm((8, 128), f32),
                vm((2, STEPS, ROWS, 128), f32),
                vm((2, STEPS, ROWS, 128), f32),
                vm((2, STEPS, 3, 8, 128), f32),
                vm((2, STEPS, 3, 8, 128), f32),
                vm((4, 8, 128), f32),
                vm((4, 8, 128), f32),
                vm((2, 3, 4, 17, 128), f32),
                vm((1, 2, 128), f32),
                dma((9,)),
                dma((9,)),
                dma((9,)),
                dma((2, STEPS)),
                dma((2, STEPS)),
                dma((2, STEPS)),
                dma((2, STEPS)),
                dma((4,)),
                dma((4,)),
                dma((3,)),
            ],
            compiler_params=pltpu.CompilerParams(collective_id=0, has_side_effects=True),
        )(now, nxt, lam, mu, dens, flags, slope, ns, owner)

    return jax.shard_map(
        on_device,
        mesh=mesh,
        in_specs=(
            P(None, "dom", "depth", None),
            P(None, "dom", "depth", None),
            P("dom", "depth", None),
            P("dom", "depth", None),
            P("dom", "depth", None),
            P(None, "depth", "dom", None),
            P("depth", "dom", None),
            P("depth", "dom", None),
            P("depth", "dom"),
        ),
        out_specs=(
            P(None, "dom", "depth", None),
            P(None, "dom", "depth", None),
            P("depth", "dom", None),
        ),
        check_vma=False,
    )
```

```python
import functools
import math

import jax
import jax.numpy as jnp
import numpy as np
from jax import lax
from jax.experimental import pallas as pl
from jax.experimental.pallas import tpu as pltpu
from jax.sharding import PartitionSpec as P


MESH = pl.DeviceIdType.MESH
STEPS = 4
ROWS = 80
DT2 = 0.01 * 0.01
LOCK = 0.5
W5 = [0.1, 49.0 / 90.0, 32.0 / 45.0, 49.0 / 90.0, 0.1]
OFFSETS = (-2, -1, 1, 2)
f32 = jnp.float32


def slopes5():
    pts = [-1.0, -math.sqrt(3.0 / 7.0), 0.0, math.sqrt(3.0 / 7.0), 1.0]
    prod = [np.prod([pts[a] - pts[b] for b in range(5) if b != a]) for a in range(5)]
    d = np.zeros((5, 5))
    for a in range(5):
        for b in range(5):
            if a == b:
                d[a, b] = sum(1.0 / (pts[a] - pts[o]) for o in range(5) if o != a)
            else:
                d[a, b] = prod[a] / prod[b] / (pts[a] - pts[b])
    d[2, 2] = 0.0
    return 2.0 * d


D5 = slopes5()


def apply5(m, v):
    e0, e1, o0, o1 = v[0] + v[4], v[1] + v[3], v[0] - v[4], v[1] - v[3]
    out = [None] * 5
    for q in (0, 1):
        a = (
            float((m[q, 0] + m[q, 4]) / 2) * e0
            + float((m[q, 1] + m[q, 3]) / 2) * e1
            + float(m[q, 2]) * v[2]
        )
        b = float((m[q, 0] - m[q, 4]) / 2) * o0 + float((m[q, 1] - m[q, 3]) / 2) * o1
        out[q] = b + a
        out[4 - q] = b - a
    out[2] = float((m[2, 0] - m[2, 4]) / 2) * o0 + float((m[2, 1] - m[2, 3]) / 2) * o1
    return out


def wkey(a, b):
    a, b = min(a, 4 - a), min(b, 4 - b)
    a, b = min(a, b), max(a, b)
    return {(0, 0): 0, (0, 1): 1, (0, 2): 2, (1, 1): 3, (1, 2): 4, (2, 2): 5}[(a, b)]


WPAIR = [(0, 0), (0, 1), (0, 2), (1, 1), (1, 2), (2, 2)]


def rblk(c, yl, zl):
    return (c * 5 + yl) * 5 + zl


def kernel(
    nd,
    ndp,
    now,
    nxt,
    lam,
    mu,
    dens,
    flags,
    slope,
    ns,
    owner,
    out_cur,
    out_fol,
    out_patch,
    nowv,
    nxtv,
    densv,
    modv,
    flagv,
    slopev,
    nsv,
    ownv,
    gflag,
    gslope,
    S,
    F,
    GY,
    FX,
    FY,
    IM,
    IMP,
    CONST,
    TH,
    grad,
    send_dom,
    recv_dom,
    send_dep,
    recv_dep,
    psend,
    precv,
    outv,
    patchv,
    lsem,
    isend,
    irecv,
    dsend,
    drecv,
    fsend,
    frecv,
    pss,
    prs,
    osem,
):
    me = lax.axis_index("dom")
    my = lax.axis_index("depth")
    up = lax.rem(my + 1, ndp)
    dn = lax.rem(my + ndp - 1, ndp)
    has_l = me > 0
    has_r = me < nd - 1
    odd = lax.rem(me, 2) == 1

    barrier = pltpu.get_barrier_semaphore()
    count = 2
    for off, row in ((-1, my), (1, my), (-2, my), (2, my), (-1, up), (1, dn)):
        ok = jnp.logical_and(me + off >= 0, me + off < nd)
        count = count + ok.astype(jnp.int32)

        @pl.when(ok)
        def _(off=off, row=row):
            pl.semaphore_signal(
                barrier, inc=1, device_id=(me + off, row), device_id_type=MESH
            )

    pl.semaphore_signal(barrier, inc=1, device_id=(me, up), device_id_type=MESH)
    pl.semaphore_signal(barrier, inc=1, device_id=(me, dn), device_id_type=MESH)

    locals_ = [
        pltpu.make_async_copy(a, b, lsem.at[i])
        for i, (a, b) in enumerate(
            [
                (now, nowv.at[0, :, :, 0:4, :]),
                (now.at[:, :, 0:1, :], nowv.at[1, :, :, 4:5, :]),
                (lam, modv.at[0, 0]),
                (mu, modv.at[0, 1]),
                (nxt, nxtv.at[:, :, 0:4, :]),
                (dens, densv.at[:, 0:4, :]),
                (flags, flagv),
                (slope, slopev),
                (ns, nsv),
                (owner, ownv),
            ]
        )
    ]
    for cp in locals_:
        cp.start()
    pl.semaphore_wait(barrier, count)

    def remote(i, src, dst, to):
        return pltpu.make_async_remote_copy(
            src_ref=src,
            dst_ref=dst,
            send_sem=isend.at[i],
            recv_sem=irecv.at[i],
            device_id=to,
            device_id_type=MESH,
        )

    to_left = [
        remote(0, now.at[:, :, 0:1, :], nowv.at[0, :, :, 4:5, :], (me - 1, my)),
        remote(1, nxt.at[:, :, 0:1, :], nxtv.at[:, :, 4:5, :], (me - 1, my)),
        remote(2, dens.at[:, 0:1, :], densv.at[:, 4:5, :], (me - 1, my)),
        remote(3, flags, gflag.at[0], (me - 1, my)),
        remote(4, slope, gslope.at[0], (me - 1, my)),
        remote(5, flags, gflag.at[1], (me - 1, up)),
        remote(6, slope, gslope.at[1], (me - 1, up)),
    ]
    to_up = [
        remote(7, flags, gflag.at[2], (me, up)),
        remote(8, slope, gslope.at[2], (me, up)),
    ]
    to_right = [
        remote(9, now, nowv.at[1, :, :, 0:4, :], (me + 1, my)),
        remote(10, lam, modv.at[1, 0], (me + 1, my)),
        remote(11, mu, modv.at[1, 1], (me + 1, my)),
    ]

    @pl.when(has_l)
    def _():
        to_left[0].start()

    @pl.when(has_r)
    def _():
        for cp in to_right:
            cp.start()

    @pl.when(has_l)
    def _():
        for cp in to_left[1:]:
            cp.start()

    for cp in to_up:
        cp.start()

    lane = lax.broadcasted_iota(jnp.int32, (8, 128), 1)
    sub = lax.broadcasted_iota(jnp.int32, (8, 128), 0)
    blk = lane // 32
    ez = lane % 32
    to_packed = 4 * ez + blk
    to_natural = (lane % 4) * 32 + lane // 4
    b0, b1, b2, b3 = blk == 0, blk == 1, blk == 2, blk == 3

    def permute(x, idx):
        return jnp.take_along_axis(x, idx, axis=1)

    def roll(x, shift):
        shift = shift % 128
        return x if shift == 0 else pltpu.roll(x, shift, 1)

    def by_sub(vals):
        v = jnp.full((8, 128), 0.0, f32)
        for i, x in enumerate(vals):
            if x != 0.0:
                v = jnp.where(sub == i, float(x), v)
        return v

    for k in range(5):
        CONST[k] = by_sub(D5[:, k])
        CONST[5 + k] = by_sub(D5[k, :])

    for i in range(75, ROWS):
        for slot in range(2):
            F[slot, pl.ds(8 * i, 8), :] = jnp.zeros((8, 128), f32)
            S[slot, pl.ds(8 * i, 8), :] = jnp.zeros((8, 128), f32)

    live_x = jnp.logical_or(sub < 4, jnp.logical_and(sub == 4, has_r))

    def pick(r0, r1, r2, r3):
        return jnp.where(b0, r0, jnp.where(b1, r1, jnp.where(b2, r2, r3)))

    def to_elements(load, put, bottom):
        packed = [permute(load(y), to_packed) for y in range(17)]
        rolled = [[roll(v, 32 * s) for s in range(4)] for v in packed]
        for yl in range(5):
            for zl in range(4):
                v = pick(*[rolled[4 * e + yl][(e - zl) % 4] for e in range(4)])
                put(yl, zl, v)
                if zl == 0:
                    first = v
            put(yl, 4, jnp.where(ez == 31, bottom, roll(first, -1)))

    def wide(slot, which):
        z = jnp.zeros((1, 96), f32)
        out = jnp.zeros((8, 128), f32)
        for e in range(4):
            row = jnp.concatenate([modv[slot, which, 0, pl.ds(e, 1), :], z], axis=1)
            row = jnp.broadcast_to(row, (8, 128))
            out = jnp.where(blk == e, roll(row, 32 * e), out)
        return out

    def put_moduli(slot):
        wq = by_sub([w / 8.0 for w in W5])
        for j in range(2):
            m = wide(slot, j) * wq
            for i, (a, b) in enumerate(WPAIR):
                CONST[10 + 12 * slot + 6 * j + i] = m * float(W5[a] * W5[b])

    def mass_table():
        wx = by_sub([0.2, W5[1], W5[2], W5[3], 0.2])
        wx = jnp.where(sub == 0, jnp.where(has_l, 0.2, 0.1), wx)

        def put_mass(yl, zl, v):
            if yl in (1, 2, 3):
                wy = W5[yl]
            else:
                wy = jnp.where(b0 if yl == 0 else b3, 0.1, 0.2)
            if zl in (1, 2, 3):
                wz = W5[zl]
            elif zl == 0:
                wz = jnp.where(ez == 0, 0.1, 0.2)
            else:
                wz = 0.2
            mass = v * wx * wy * wz
            live = jnp.logical_and(live_x, ez < 31) if zl == 4 else live_x
            IM[pl.ds(8 * (yl * 5 + zl), 8), :] = jnp.where(
                live, (8.0 * DT2) / jnp.where(live, mass, 1.0), 0.0
            )

        to_elements(lambda y: jnp.where(live_x, densv[y], 1.0), put_mass, 1.0)
        for c in range(3):
            for i in range(25):
                IMP[0, pl.ds(25 * c + i, 1), :] = IM[pl.ds(8 * i, 1), :]
                IMP[1, pl.ds(25 * c + i, 1), :] = IM[pl.ds(8 * i + 4, 1), :]
        for i in range(75, ROWS):
            IMP[0, pl.ds(i, 1), :] = jnp.zeros((1, 128), f32)
            IMP[1, pl.ds(i, 1), :] = jnp.zeros((1, 128), f32)

    def following_field():
        for c in range(3):

            def put(yl, zl, v, c=c):
                S[1, pl.ds(8 * rblk(c, yl, zl), 8), :] = v

            to_elements(lambda y, c=c: jnp.where(live_x, nxtv[c, y], 0.0), put, 0.0)

    def fault_tables():
        def planes(own, ghost):
            top = jnp.concatenate([own, jnp.zeros((4, 128), own.dtype)], axis=0)
            low = jnp.concatenate([ghost, ghost], axis=0)
            return jnp.where(sub == 4, low, top)

        def spread(ghost):
            return jnp.broadcast_to(ghost[0:1], (4, 128))

        own_s = planes(slopev[0], spread(gslope[0, 0]))
        low_s = planes(gslope[2, 0], spread(gslope[1, 0]))
        stress = jnp.concatenate([nsv[0], jnp.zeros((4, 128), f32)], axis=0)
        for i in range(STEPS):
            own_f = planes(flagv[i, 0], spread(gflag[0, i, 0]))
            low_f = planes(gflag[2, i, 0], spread(gflag[1, i, 0]))
            for j, (fl, sl) in enumerate(((own_f, own_s), (low_f, low_s))):
                t = jnp.where(fl == 0, LOCK, jnp.where(fl == 1, -sl, 0.0))
                TH[j, i] = permute(jnp.where(live_x, t, 0.0), to_packed)
            h = jnp.where(own_f == 1, 0.5, jnp.where(own_f == 2, 1.0, 0.0))
            TH[2, i] = permute(jnp.where(sub < 4, h * stress, 0.0), to_packed)

    def dom_copy(side, step):
        to = me - 1 if side == 0 else me + 1
        return pltpu.make_async_remote_copy(
            src_ref=send_dom.at[side, step],
            dst_ref=recv_dom.at[side, step],
            send_sem=dsend.at[side, step],
            recv_sem=drecv.at[side, step],
            device_id=(to, my),
            device_id_type=MESH,
        )

    def dep_copy(side, step):
        to = dn if side == 0 else up
        return pltpu.make_async_remote_copy(
            src_ref=send_dep.at[side, step],
            dst_ref=recv_dep.at[side, step],
            send_sem=fsend.at[side, step],
            recv_sem=frecv.at[side, step],
            device_id=(me, to),
            device_id_type=MESH,
        )

    def patch_copy(i):
        return pltpu.make_async_remote_copy(
            src_ref=psend.at[i],
            dst_ref=precv.at[i],
            send_sem=pss.at[i],
            recv_sem=prs.at[i],
            device_id=(me + OFFSETS[i], my),
            device_id_type=MESH,
        )

    def inside(v):
        return jnp.logical_and(v >= 0, v < nd)

    def send_patches():
        total = permute(grad[...], to_natural)
        rows = [total[x : x + 1] for x in range(4)]

        def members(off, p):
            num = (me + off) * 2 + p
            acc = jnp.zeros((1, 128), f32)
            for x in range(4):
                acc = acc + jnp.where(ownv[0, x] == num, rows[x], 0.0)
            return acc

        for i, off in enumerate(OFFSETS):
            psend[i] = jnp.zeros((8, 128), f32)
            for p in range(2):
                psend[i, pl.ds(p, 1), :] = members(off, p)

            @pl.when(inside(me + off))
            def _(i=i):
                patch_copy(i).start()

        patchv[0, pl.ds(0, 1), :] = members(0, 0)
        patchv[0, pl.ds(1, 1), :] = members(0, 1)

    out_copies = [
        pltpu.make_async_copy(outv.at[0, :, :, 0:4, :], out_cur, osem.at[0]),
        pltpu.make_async_copy(outv.at[1, :, :, 0:4, :], out_fol, osem.at[1]),
        pltpu.make_async_copy(patchv, out_patch, osem.at[2]),
    ]

    def from_elements(slot, which):
        for c in range(3):

            def e(yl, zl):
                return S[slot, pl.ds(8 * rblk(c, yl, zl), 8), :]

            for y in range(17):
                ey, yl = (y // 4, y % 4) if y < 16 else (3, 4)
                v = pick(*[roll(e(yl, zl), 32 * (zl - ey)) for zl in range(4)])
                outv[which, c, y] = permute(v, to_natural)
        out_copies[which].start()

    grad[...] = jnp.zeros((8, 128), f32)

    def turn(it, carry):
        step = jnp.maximum(it - 1, 0)
        is_left = jnp.logical_or(
            jnp.logical_and(it == 0, odd),
            jnp.logical_and(it == 1, jnp.logical_not(odd)),
        )
        own = jnp.logical_not(is_left)
        cur = lax.rem(step, 2)
        new = 1 - cur
        fs = is_left.astype(jnp.int32)
        src = cur + 2 * fs
        cb = 10 + 12 * fs

        @pl.when(it < 2)
        def _():
            @pl.when(is_left)
            def _():
                locals_[1].wait()

                @pl.when(has_l)
                def _():
                    for cp in to_right:
                        cp.wait_recv()

                put_moduli(1)

            @pl.when(own)
            def _():
                for cp in (locals_[0], locals_[2], locals_[3]):
                    cp.wait()
                put_moduli(0)

                @pl.when(has_r)
                def _():
                    to_left[0].wait_recv()

            live = jnp.logical_or(
                sub < 4, jnp.logical_and(sub == 4, jnp.logical_or(is_left, has_r))
            )
            for c in range(3):

                def put(yl, zl, v, c=c):
                    S[src, pl.ds(8 * rblk(c, yl, zl), 8), :] = v

                to_elements(
                    lambda y, c=c: jnp.where(live, nowv[fs, c, y], 0.0), put, 0.0
                )

        def u(c, yl, zl):
            return S[src, pl.ds(8 * rblk(c, yl, zl), 8), :]

        @pl.when(own)
        def _():
            for c in range(3):
                low = [roll(u(c, 0, z), 32 * z) for z in range(4)]
                high = [roll(u(c, 4, z), 32 * (z - 3)) for z in range(4)]
                send_dep[0, step, c] = pick(*low)
                send_dep[1, step, c] = pick(*high)
            dep_copy(0, step).start()
            dep_copy(1, step).start()

        for c in range(3):
            for zl in range(5):
                g = apply5(D5, [u(c, yl, zl) for yl in range(5)])
                for yl in range(5):
                    GY[pl.ds(8 * rblk(c, yl, zl), 8), :] = g[yl]
        for yl in range(5):
            gz = [apply5(D5, [u(c, yl, zl) for zl in range(5)]) for c in range(3)]
            fz = [[None] * 5 for _ in range(3)]
            for zl in range(5):
                gx, gy = [], []
                for c in range(3):
                    r = 8 * rblk(c, yl, zl)
                    acc = None
                    for k in range(5):
                        row = jnp.broadcast_to(S[src, pl.ds(r + k, 1), :], (8, 128))
                        t = row * CONST[k]
                        acc = t if acc is None else acc + t
                    gx.append(acc)
                    gy.append(GY[pl.ds(r, 8), :])
                key = wkey(yl, zl)
                lw, mw = CONST[cb + key], CONST[cb + 6 + key]
                m2 = mw + mw
                common = lw * (gx[0] + gy[1] + gz[2][zl])
                sxx = common + m2 * gx[0]
                syy = common + m2 * gy[1]
                szz = common + m2 * gz[2][zl]
                sxy = mw * (gx[1] + gy[0])
                sxz = mw * (gx[2] + gz[0][zl])
                syz = mw * (gy[2] + gz[1][zl])
                for c, (vx, vy, vz) in enumerate(
                    ((sxx, sxy, sxz), (sxy, syy, syz), (sxz, syz, szz))
                ):
                    r = 8 * rblk(c, yl, zl)
                    FX[pl.ds(r, 8), :] = vx
                    FY[pl.ds(r, 8), :] = vy
                    fz[c][zl] = vz
            for c in range(3):
                back = apply5(D5.T, fz[c])
                for zl in range(5):
                    F[fs, pl.ds(8 * rblk(c, yl, zl), 8), :] = back[zl]
        for c in range(3):
            for zl in range(5):
                rs = [8 * rblk(c, yl, zl) for yl in range(5)]
                back = apply5(D5.T, [FY[pl.ds(r, 8), :] for r in rs])
                for yl, r in enumerate(rs):
                    acc = back[yl] + F[fs, pl.ds(r, 8), :]
                    for q in range(5):
                        row = jnp.broadcast_to(FX[pl.ds(r + q, 1), :], (8, 128))
                        acc = acc + row * CONST[5 + q]
                    F[fs, pl.ds(r, 8), :] = acc

        for c in range(3):
            for yl in range(5):
                ra, rb = pl.ds(8 * rblk(c, yl, 0), 8), pl.ds(8 * rblk(c, yl, 4), 8)
                fa, fb = F[fs, ra, :], F[fs, rb, :]
                F[fs, ra, :] = fa + jnp.where(ez == 0, 0.0, roll(fb, 1))
                F[fs, rb, :] = fb + roll(fa, -1)
        for c in range(3):
            for zl in range(5):
                ra, rb = pl.ds(8 * rblk(c, 0, zl), 8), pl.ds(8 * rblk(c, 4, zl), 8)
                fa, fb = F[fs, ra, :], F[fs, rb, :]
                F[fs, ra, :] = fa + jnp.where(b0, 0.0, roll(fb, 32))
                F[fs, rb, :] = fb + jnp.where(b3, 0.0, roll(fa, -32))

        @pl.when(is_left)
        def _():
            for g in range(ROWS // 8):
                recv_dom[1, 0, pl.ds(8 * g, 8), :] = F[1, pl.ds(64 * g + 4, 8, stride=8), :]

        @pl.when(own)
        def _():
            for g in range(ROWS // 8):
                d = pl.ds(8 * g, 8)
                send_dom[0, step, d, :] = F[0, pl.ds(64 * g, 8, stride=8), :]
                send_dom[1, step, d, :] = F[0, pl.ds(64 * g + 4, 8, stride=8), :]

            @pl.when(has_l)
            def _():
                dom_copy(0, step).start()

            @pl.when(jnp.logical_and(has_r, step > 0))
            def _():
                dom_copy(1, step).start()

        @pl.when(it == 1)
        def _():
            for cp in locals_[4:]:
                cp.wait()
            for cp in to_up:
                cp.wait_recv()

            @pl.when(has_r)
            def _():
                for cp in to_left[1:]:
                    cp.wait_recv()

            following_field()
            mass_table()
            fault_tables()

        @pl.when(it > 0)
        def _():
            dep_copy(0, step).wait_recv()
            dep_copy(1, step).wait_recv()
            for c in range(3):
                slip_hi = recv_dep[0, step, c] - send_dep[1, step, c]
                slip_lo = send_dep[0, step, c] - recv_dep[1, step, c]
                if c == 0:
                    grad[...] = grad[...] + TH[2, step] * slip_hi
                hi = (LOCK if c == 1 else TH[0, step]) * slip_hi
                lo = (LOCK if c == 1 else TH[1, step]) * slip_lo
                for zl in range(5):
                    sh = (96, 0) if zl < 4 else (95, -1)
                    zb = zl if zl < 4 else 0
                    rh, rl = pl.ds(8 * rblk(c, 4, zl), 8), pl.ds(8 * rblk(c, 0, zl), 8)
                    F[0, rh, :] = F[0, rh, :] - jnp.where(
                        b3, roll(hi, sh[0] - 32 * zb), 0.0
                    )
                    F[0, rl, :] = F[0, rl, :] + jnp.where(
                        b0, roll(lo, sh[1] - 32 * zb), 0.0
                    )

            for yl in range(5):
                for zl in range(5):
                    im = IM[pl.ds(8 * (yl * 5 + zl), 8), :]
                    for c in range(3):
                        r = pl.ds(8 * rblk(c, yl, zl), 8)
                        now_u = S[cur, r, :]
                        S[new, r, :] = (now_u + now_u) - S[new, r, :] - im * F[0, r, :]

            @pl.when(it == STEPS)
            def _():
                send_patches()
                from_elements(1 - STEPS % 2, 1)

            def add_side(side, first):
                plane = 0 if first == 0 else 1
                for g in range(ROWS // 8):
                    r = pl.ds(64 * g + first, 8, stride=8)
                    d = pl.ds(8 * g, 8)
                    S[new, r, :] = S[new, r, :] - IMP[plane, d, :] * recv_dom[side, step, d, :]

            @pl.when(has_r)
            def _():
                dom_copy(0, step).wait_recv()
                add_side(0, 4)

            @pl.when(has_l)
            def _():
                @pl.when(step > 0)
                def _():
                    dom_copy(1, step).wait_recv()

                add_side(1, 0)

        return carry

    lax.fori_loop(0, STEPS + 1, turn, 0)

    from_elements(STEPS % 2, 0)
    for i, off in enumerate(OFFSETS):

        @pl.when(inside(me - off))
        def _(i=i):
            patch_copy(i).wait_recv()
            patchv[0] = patchv[0] + precv[i, pl.ds(0, 2), :]

    out_copies[2].start()

    @pl.when(has_l)
    def _():
        for cp in to_left:
            cp.wait_send()
        for s in range(STEPS):
            dom_copy(0, s).wait_send()

    @pl.when(has_r)
    def _():
        for cp in to_right:
            cp.wait_send()
        for s in range(1, STEPS):
            dom_copy(1, s).wait_send()

    for cp in to_up:
        cp.wait_send()
    for s in range(STEPS):
        dep_copy(0, s).wait_send()
        dep_copy(1, s).wait_send()
    for i, off in enumerate(OFFSETS):

        @pl.when(inside(me + off))
        def _(i=i):
            patch_copy(i).wait_send()

    for cp in out_copies:
        cp.wait()


def solution(mesh):
    nd, ndp = mesh.shape["dom"], mesh.shape["depth"]

    def on_device(now, nxt, lam, mu, dens, flags, slope, ns, owner):
        any_ = pl.BlockSpec(memory_space=pl.ANY)
        dma = pltpu.SemaphoreType.DMA
        vm = pltpu.VMEM
        i32 = jnp.int32
        cur, fol, patch = pl.pallas_call(
            functools.partial(kernel, nd, ndp),
            name="rupture",
            out_shape=(
                jax.ShapeDtypeStruct((3, 17, 4, 128), f32),
                jax.ShapeDtypeStruct((3, 17, 4, 128), f32),
                jax.ShapeDtypeStruct((1, 2, 128), f32),
            ),
            in_specs=[any_] * 9,
            out_specs=[any_] * 3,
            scratch_shapes=[
                vm((2, 3, 17, 8, 128), f32),
                vm((3, 17, 8, 128), f32),
                vm((17, 8, 128), f32),
                vm((2, 2, 1, 4, 32), f32),
                vm((4, 1, 4, 128), i32),
                vm((1, 4, 128), f32),
                vm((1, 4, 128), f32),
                pltpu.SMEM((1, 4), i32),
                vm((3, 4, 1, 4, 128), i32),
                vm((3, 1, 4, 128), f32),
                vm((3, ROWS * 8, 128), f32),
                vm((2, ROWS * 8, 128), f32),
                vm((ROWS * 8, 128), f32),
                vm((ROWS * 8, 128), f32),
                vm((ROWS * 8, 128), f32),
                vm((25 * 8, 128), f32),
                vm((2, ROWS, 128), f32),
                vm((34, 8, 128), f32),
                vm((3, STEPS, 8, 128), f32),
                vm((8, 128), f32),
                vm((2, STEPS, ROWS, 128), f32),
                vm((2, STEPS, ROWS, 128), f32),
                vm((2, STEPS, 3, 8, 128), f32),
                vm((2, STEPS, 3, 8, 128), f32),
                vm((4, 8, 128), f32),
                vm((4, 8, 128), f32),
                vm((2, 3, 17, 8, 128), f32),
                vm((1, 2, 128), f32),
                dma((10,)),
                dma((12,)),
                dma((12,)),
                dma((2, STEPS)),
                dma((2, STEPS)),
                dma((2, STEPS)),
                dma((2, STEPS)),
                dma((4,)),
                dma((4,)),
                dma((3,)),
            ],
            compiler_params=pltpu.CompilerParams(collective_id=0, has_side_effects=True),
        )(
            jnp.transpose(now, (0, 2, 1, 3)),
            jnp.transpose(nxt, (0, 2, 1, 3)),
            lam,
            mu,
            jnp.transpose(dens, (1, 0, 2)),
            flags,
            slope,
            ns,
            owner,
        )
        return jnp.transpose(cur, (0, 2, 1, 3)), jnp.transpose(fol, (0, 2, 1, 3)), patch

    return jax.shard_map(
        on_device,
        mesh=mesh,
        in_specs=(
            P(None, "dom", "depth", None),
            P(None, "dom", "depth", None),
            P("dom", "depth", None),
            P("dom", "depth", None),
            P("dom", "depth", None),
            P(None, "depth", "dom", None),
            P("depth", "dom", None),
            P("depth", "dom", None),
            P("depth", "dom"),
        ),
        out_specs=(
            P(None, "dom", "depth", None),
            P(None, "dom", "depth", None),
            P("depth", "dom", None),
        ),
        check_vma=False,
    )
```

```python
import functools
import math

import jax
import jax.numpy as jnp
import numpy as np
from jax import lax
from jax.experimental import pallas as pl
from jax.experimental.pallas import tpu as pltpu
from jax.sharding import PartitionSpec as P


MESH = pl.DeviceIdType.MESH
STEPS = 4
ROWS = 80
DT2 = 0.01 * 0.01
LOCK = 0.5
W5 = [0.1, 49.0 / 90.0, 32.0 / 45.0, 49.0 / 90.0, 0.1]
OFFSETS = (-2, -1, 1, 2)
f32 = jnp.float32


def slopes5():
    pts = [-1.0, -math.sqrt(3.0 / 7.0), 0.0, math.sqrt(3.0 / 7.0), 1.0]
    prod = [np.prod([pts[a] - pts[b] for b in range(5) if b != a]) for a in range(5)]
    d = np.zeros((5, 5))
    for a in range(5):
        for b in range(5):
            if a == b:
                d[a, b] = sum(1.0 / (pts[a] - pts[o]) for o in range(5) if o != a)
            else:
                d[a, b] = prod[a] / prod[b] / (pts[a] - pts[b])
    d[2, 2] = 0.0
    return 2.0 * d


D5 = slopes5()


def apply5(m, v):
    e0, e1, o0, o1 = v[0] + v[4], v[1] + v[3], v[0] - v[4], v[1] - v[3]
    out = [None] * 5
    for q in (0, 1):
        a = (
            float((m[q, 0] + m[q, 4]) / 2) * e0
            + float((m[q, 1] + m[q, 3]) / 2) * e1
            + float(m[q, 2]) * v[2]
        )
        b = float((m[q, 0] - m[q, 4]) / 2) * o0 + float((m[q, 1] - m[q, 3]) / 2) * o1
        out[q] = b + a
        out[4 - q] = b - a
    out[2] = float((m[2, 0] - m[2, 4]) / 2) * o0 + float((m[2, 1] - m[2, 3]) / 2) * o1
    return out


def wkey(a, b):
    a, b = min(a, 4 - a), min(b, 4 - b)
    a, b = min(a, b), max(a, b)
    return {(0, 0): 0, (0, 1): 1, (0, 2): 2, (1, 1): 3, (1, 2): 4, (2, 2): 5}[(a, b)]


WPAIR = [(0, 0), (0, 1), (0, 2), (1, 1), (1, 2), (2, 2)]


def rblk(c, yl, zl):
    return (c * 5 + yl) * 5 + zl


def kernel(
    nd,
    ndp,
    now,
    nxt,
    lam,
    mu,
    dens,
    flags,
    slope,
    ns,
    owner,
    out_cur,
    out_fol,
    out_patch,
    nowv,
    nxtv,
    densv,
    modv,
    flagv,
    slopev,
    nsv,
    ownv,
    gflag,
    gslope,
    S,
    F,
    GY,
    FX,
    FY,
    IM,
    IMP,
    CONST,
    TH,
    grad,
    send_dom,
    recv_dom,
    send_dep,
    recv_dep,
    psend,
    precv,
    lsem,
    isend,
    irecv,
    dsend,
    drecv,
    fsend,
    frecv,
    pss,
    prs,
):
    me = lax.axis_index("dom")
    my = lax.axis_index("depth")
    up = lax.rem(my + 1, ndp)
    dn = lax.rem(my + ndp - 1, ndp)
    has_l = me > 0
    has_r = me < nd - 1
    odd = lax.rem(me, 2) == 1

    barrier = pltpu.get_barrier_semaphore()
    count = 2
    for off, row in ((-1, my), (1, my), (-2, my), (2, my), (-1, up), (1, dn)):
        ok = jnp.logical_and(me + off >= 0, me + off < nd)
        count = count + ok.astype(jnp.int32)

        @pl.when(ok)
        def _(off=off, row=row):
            pl.semaphore_signal(
                barrier, inc=1, device_id=(me + off, row), device_id_type=MESH
            )

    pl.semaphore_signal(barrier, inc=1, device_id=(me, up), device_id_type=MESH)
    pl.semaphore_signal(barrier, inc=1, device_id=(me, dn), device_id_type=MESH)

    locals_ = [
        pltpu.make_async_copy(a, b, lsem.at[i])
        for i, (a, b) in enumerate(
            [
                (now, nowv.at[0, :, :, 0:4, :]),
                (now.at[:, :, 0:1, :], nowv.at[1, :, :, 4:5, :]),
                (lam, modv.at[0, 0]),
                (mu, modv.at[0, 1]),
                (nxt, nxtv.at[:, :, 0:4, :]),
                (dens, densv.at[:, 0:4, :]),
                (flags, flagv),
                (slope, slopev),
                (ns, nsv),
                (owner, ownv),
            ]
        )
    ]
    for cp in locals_:
        cp.start()
    for cp in locals_[:4]:
        cp.wait()
    pl.semaphore_wait(barrier, count)

    def remote(i, src, dst, to):
        return pltpu.make_async_remote_copy(
            src_ref=src,
            dst_ref=dst,
            send_sem=isend.at[i],
            recv_sem=irecv.at[i],
            device_id=to,
            device_id_type=MESH,
        )

    to_left = [
        remote(0, nowv.at[0, :, :, 0:1, :], nowv.at[0, :, :, 4:5, :], (me - 1, my)),
        remote(1, nxt.at[:, :, 0:1, :], nxtv.at[:, :, 4:5, :], (me - 1, my)),
        remote(2, dens.at[:, 0:1, :], densv.at[:, 4:5, :], (me - 1, my)),
        remote(3, flags, gflag.at[0], (me - 1, my)),
        remote(4, slope, gslope.at[0], (me - 1, my)),
        remote(5, flags, gflag.at[1], (me - 1, up)),
        remote(6, slope, gslope.at[1], (me - 1, up)),
    ]
    to_up = [
        remote(7, flags, gflag.at[2], (me, up)),
        remote(8, slope, gslope.at[2], (me, up)),
    ]
    to_right = [
        remote(9, nowv.at[0, :, :, 0:4, :], nowv.at[1, :, :, 0:4, :], (me + 1, my)),
        remote(10, lam, modv.at[1, 0], (me + 1, my)),
        remote(11, mu, modv.at[1, 1], (me + 1, my)),
    ]

    @pl.when(has_l)
    def _():
        to_left[0].start()

    @pl.when(has_r)
    def _():
        for cp in to_right:
            cp.start()

    @pl.when(has_l)
    def _():
        for cp in to_left[1:]:
            cp.start()

    for cp in to_up:
        cp.start()

    lane = lax.broadcasted_iota(jnp.int32, (8, 128), 1)
    sub = lax.broadcasted_iota(jnp.int32, (8, 128), 0)
    blk = lane // 32
    ez = lane % 32
    to_packed = 4 * ez + blk
    to_natural = (lane % 4) * 32 + lane // 4
    b0, b1, b2, b3 = blk == 0, blk == 1, blk == 2, blk == 3

    def permute(x, idx):
        return jnp.take_along_axis(x, idx, axis=1)

    def roll(x, shift):
        shift = shift % 128
        return x if shift == 0 else pltpu.roll(x, shift, 1)

    def by_sub(vals):
        v = jnp.full((8, 128), 0.0, f32)
        for i, x in enumerate(vals):
            if x != 0.0:
                v = jnp.where(sub == i, float(x), v)
        return v

    for k in range(5):
        CONST[k] = by_sub(D5[:, k])
        CONST[5 + k] = by_sub(D5[k, :])

    for i in range(75, ROWS):
        for slot in range(2):
            F[slot, pl.ds(8 * i, 8), :] = jnp.zeros((8, 128), f32)
            S[slot, pl.ds(8 * i, 8), :] = jnp.zeros((8, 128), f32)

    live_x = jnp.logical_or(sub < 4, jnp.logical_and(sub == 4, has_r))

    def pick(r0, r1, r2, r3):
        return jnp.where(b0, r0, jnp.where(b1, r1, jnp.where(b2, r2, r3)))

    def to_elements(load, put, bottom):
        packed = [permute(load(y), to_packed) for y in range(17)]
        rolled = [[roll(v, 32 * s) for s in range(4)] for v in packed]
        for yl in range(5):
            for zl in range(4):
                v = pick(*[rolled[4 * e + yl][(e - zl) % 4] for e in range(4)])
                put(yl, zl, v)
                if zl == 0:
                    first = v
            put(yl, 4, jnp.where(ez == 31, bottom, roll(first, -1)))

    def wide(slot, which):
        z = jnp.zeros((1, 96), f32)
        out = jnp.zeros((8, 128), f32)
        for e in range(4):
            row = jnp.concatenate([modv[slot, which, 0, pl.ds(e, 1), :], z], axis=1)
            row = jnp.broadcast_to(row, (8, 128))
            out = jnp.where(blk == e, roll(row, 32 * e), out)
        return out

    def put_moduli(slot):
        wq = by_sub([w / 8.0 for w in W5])
        for j in range(2):
            m = wide(slot, j) * wq
            for i, (a, b) in enumerate(WPAIR):
                CONST[10 + 12 * slot + 6 * j + i] = m * float(W5[a] * W5[b])

    def mass_table():
        wx = by_sub([0.2, W5[1], W5[2], W5[3], 0.2])
        wx = jnp.where(sub == 0, jnp.where(has_l, 0.2, 0.1), wx)

        def put_mass(yl, zl, v):
            if yl in (1, 2, 3):
                wy = W5[yl]
            else:
                wy = jnp.where(b0 if yl == 0 else b3, 0.1, 0.2)
            if zl in (1, 2, 3):
                wz = W5[zl]
            elif zl == 0:
                wz = jnp.where(ez == 0, 0.1, 0.2)
            else:
                wz = 0.2
            mass = v * wx * wy * wz
            live = jnp.logical_and(live_x, ez < 31) if zl == 4 else live_x
            IM[pl.ds(8 * (yl * 5 + zl), 8), :] = jnp.where(
                live, (8.0 * DT2) / jnp.where(live, mass, 1.0), 0.0
            )

        to_elements(lambda y: jnp.where(live_x, densv[y], 1.0), put_mass, 1.0)
        for c in range(3):
            for i in range(25):
                IMP[0, pl.ds(25 * c + i, 1), :] = IM[pl.ds(8 * i, 1), :]
                IMP[1, pl.ds(25 * c + i, 1), :] = IM[pl.ds(8 * i + 4, 1), :]
        for i in range(75, ROWS):
            IMP[0, pl.ds(i, 1), :] = jnp.zeros((1, 128), f32)
            IMP[1, pl.ds(i, 1), :] = jnp.zeros((1, 128), f32)

    def following_field():
        for c in range(3):

            def put(yl, zl, v, c=c):
                S[1, pl.ds(8 * rblk(c, yl, zl), 8), :] = v

            to_elements(lambda y, c=c: jnp.where(live_x, nxtv[c, y], 0.0), put, 0.0)

    def fault_tables():
        def planes(own, ghost):
            top = jnp.concatenate([own, jnp.zeros((4, 128), own.dtype)], axis=0)
            low = jnp.concatenate([ghost, ghost], axis=0)
            return jnp.where(sub == 4, low, top)

        def spread(ghost):
            return jnp.broadcast_to(ghost[0:1], (4, 128))

        own_s = planes(slopev[0], spread(gslope[0, 0]))
        low_s = planes(gslope[2, 0], spread(gslope[1, 0]))
        stress = jnp.concatenate([nsv[0], jnp.zeros((4, 128), f32)], axis=0)
        for i in range(STEPS):
            own_f = planes(flagv[i, 0], spread(gflag[0, i, 0]))
            low_f = planes(gflag[2, i, 0], spread(gflag[1, i, 0]))
            for j, (fl, sl) in enumerate(((own_f, own_s), (low_f, low_s))):
                t = jnp.where(fl == 0, LOCK, jnp.where(fl == 1, -sl, 0.0))
                TH[j, i] = permute(jnp.where(live_x, t, 0.0), to_packed)
            h = jnp.where(own_f == 1, 0.5, jnp.where(own_f == 2, 1.0, 0.0))
            TH[2, i] = permute(jnp.where(sub < 4, h * stress, 0.0), to_packed)

    def dom_copy(side, step):
        to = me - 1 if side == 0 else me + 1
        return pltpu.make_async_remote_copy(
            src_ref=send_dom.at[side, step],
            dst_ref=recv_dom.at[side, step],
            send_sem=dsend.at[side, step],
            recv_sem=drecv.at[side, step],
            device_id=(to, my),
            device_id_type=MESH,
        )

    def dep_copy(side, step):
        to = dn if side == 0 else up
        return pltpu.make_async_remote_copy(
            src_ref=send_dep.at[side, step],
            dst_ref=recv_dep.at[side, step],
            send_sem=fsend.at[side, step],
            recv_sem=frecv.at[side, step],
            device_id=(me, to),
            device_id_type=MESH,
        )

    def patch_copy(i):
        return pltpu.make_async_remote_copy(
            src_ref=psend.at[i],
            dst_ref=precv.at[i],
            send_sem=pss.at[i],
            recv_sem=prs.at[i],
            device_id=(me + OFFSETS[i], my),
            device_id_type=MESH,
        )

    def inside(v):
        return jnp.logical_and(v >= 0, v < nd)

    def send_patches():
        total = permute(grad[...], to_natural)
        rows = [total[x : x + 1] for x in range(4)]

        def members(off, p):
            num = (me + off) * 2 + p
            acc = jnp.zeros((1, 128), f32)
            for x in range(4):
                acc = acc + jnp.where(ownv[0, x] == num, rows[x], 0.0)
            return acc

        for i, off in enumerate(OFFSETS):
            psend[i] = jnp.zeros((8, 128), f32)
            for p in range(2):
                psend[i, pl.ds(p, 1), :] = members(off, p)

            @pl.when(inside(me + off))
            def _(i=i):
                patch_copy(i).start()

        out_patch[0, pl.ds(0, 1), :] = members(0, 0)
        out_patch[0, pl.ds(1, 1), :] = members(0, 1)

    outs = (out_cur, out_fol)

    def from_elements(slot, which):
        for c in range(3):

            def e(yl, zl):
                return S[slot, pl.ds(8 * rblk(c, yl, zl), 8), :]

            for y in range(17):
                ey, yl = (y // 4, y % 4) if y < 16 else (3, 4)
                v = pick(*[roll(e(yl, zl), 32 * (zl - ey)) for zl in range(4)])
                outs[which][c, y] = permute(v, to_natural)[0:4]

    grad[...] = jnp.zeros((8, 128), f32)

    def turn(it, carry):
        step = jnp.maximum(it - 1, 0)
        is_left = jnp.logical_or(
            jnp.logical_and(it == 0, odd),
            jnp.logical_and(it == 1, jnp.logical_not(odd)),
        )
        own = jnp.logical_not(is_left)
        cur = lax.rem(step, 2)
        new = 1 - cur
        fs = is_left.astype(jnp.int32)
        src = cur + 2 * fs
        cb = 10 + 12 * fs

        @pl.when(it < 2)
        def _():
            @pl.when(is_left)
            def _():
                @pl.when(has_l)
                def _():
                    for cp in to_right:
                        cp.wait_recv()

                put_moduli(1)

            @pl.when(own)
            def _():
                put_moduli(0)

                @pl.when(has_r)
                def _():
                    to_left[0].wait_recv()

            live = jnp.logical_or(
                sub < 4, jnp.logical_and(sub == 4, jnp.logical_or(is_left, has_r))
            )
            for c in range(3):

                def put(yl, zl, v, c=c):
                    S[src, pl.ds(8 * rblk(c, yl, zl), 8), :] = v

                to_elements(
                    lambda y, c=c: jnp.where(live, nowv[fs, c, y], 0.0), put, 0.0
                )

        def u(c, yl, zl):
            return S[src, pl.ds(8 * rblk(c, yl, zl), 8), :]

        @pl.when(own)
        def _():
            for c in range(3):
                low = [roll(u(c, 0, z), 32 * z) for z in range(4)]
                high = [roll(u(c, 4, z), 32 * (z - 3)) for z in range(4)]
                send_dep[0, step, c] = pick(*low)
                send_dep[1, step, c] = pick(*high)
            dep_copy(0, step).start()
            dep_copy(1, step).start()

        for c in range(3):
            for zl in range(5):
                g = apply5(D5, [u(c, yl, zl) for yl in range(5)])
                for yl in range(5):
                    GY[pl.ds(8 * rblk(c, yl, zl), 8), :] = g[yl]
        for yl in range(5):
            gz = [apply5(D5, [u(c, yl, zl) for zl in range(5)]) for c in range(3)]
            fz = [[None] * 5 for _ in range(3)]
            for zl in range(5):
                gx, gy = [], []
                for c in range(3):
                    r = 8 * rblk(c, yl, zl)
                    acc = None
                    for k in range(5):
                        row = jnp.broadcast_to(S[src, pl.ds(r + k, 1), :], (8, 128))
                        t = row * CONST[k]
                        acc = t if acc is None else acc + t
                    gx.append(acc)
                    gy.append(GY[pl.ds(r, 8), :])
                key = wkey(yl, zl)
                lw, mw = CONST[cb + key], CONST[cb + 6 + key]
                m2 = mw + mw
                common = lw * (gx[0] + gy[1] + gz[2][zl])
                sxx = common + m2 * gx[0]
                syy = common + m2 * gy[1]
                szz = common + m2 * gz[2][zl]
                sxy = mw * (gx[1] + gy[0])
                sxz = mw * (gx[2] + gz[0][zl])
                syz = mw * (gy[2] + gz[1][zl])
                for c, (vx, vy, vz) in enumerate(
                    ((sxx, sxy, sxz), (sxy, syy, syz), (sxz, syz, szz))
                ):
                    r = 8 * rblk(c, yl, zl)
                    FX[pl.ds(r, 8), :] = vx
                    FY[pl.ds(r, 8), :] = vy
                    fz[c][zl] = vz
            for c in range(3):
                back = apply5(D5.T, fz[c])
                for zl in range(5):
                    F[fs, pl.ds(8 * rblk(c, yl, zl), 8), :] = back[zl]
        for c in range(3):
            for zl in range(5):
                rs = [8 * rblk(c, yl, zl) for yl in range(5)]
                back = apply5(D5.T, [FY[pl.ds(r, 8), :] for r in rs])
                for yl, r in enumerate(rs):
                    acc = back[yl] + F[fs, pl.ds(r, 8), :]
                    for q in range(5):
                        row = jnp.broadcast_to(FX[pl.ds(r + q, 1), :], (8, 128))
                        acc = acc + row * CONST[5 + q]
                    F[fs, pl.ds(r, 8), :] = acc

        for c in range(3):
            for yl in range(5):
                ra, rb = pl.ds(8 * rblk(c, yl, 0), 8), pl.ds(8 * rblk(c, yl, 4), 8)
                fa, fb = F[fs, ra, :], F[fs, rb, :]
                F[fs, ra, :] = fa + jnp.where(ez == 0, 0.0, roll(fb, 1))
                F[fs, rb, :] = fb + roll(fa, -1)
        for c in range(3):
            for zl in range(5):
                ra, rb = pl.ds(8 * rblk(c, 0, zl), 8), pl.ds(8 * rblk(c, 4, zl), 8)
                fa, fb = F[fs, ra, :], F[fs, rb, :]
                F[fs, ra, :] = fa + jnp.where(b0, 0.0, roll(fb, 32))
                F[fs, rb, :] = fb + jnp.where(b3, 0.0, roll(fa, -32))

        @pl.when(is_left)
        def _():
            for g in range(ROWS // 8):
                recv_dom[1, 0, pl.ds(8 * g, 8), :] = F[1, pl.ds(64 * g + 4, 8, stride=8), :]

        @pl.when(own)
        def _():
            for g in range(ROWS // 8):
                d = pl.ds(8 * g, 8)
                send_dom[0, step, d, :] = F[0, pl.ds(64 * g, 8, stride=8), :]
                send_dom[1, step, d, :] = F[0, pl.ds(64 * g + 4, 8, stride=8), :]

            @pl.when(has_l)
            def _():
                dom_copy(0, step).start()

            @pl.when(jnp.logical_and(has_r, step > 0))
            def _():
                dom_copy(1, step).start()

        @pl.when(it == 1)
        def _():
            for cp in locals_[4:]:
                cp.wait()
            for cp in to_up:
                cp.wait_recv()

            @pl.when(has_r)
            def _():
                for cp in to_left[1:]:
                    cp.wait_recv()

            following_field()
            mass_table()
            fault_tables()

        @pl.when(it > 0)
        def _():
            dep_copy(0, step).wait_recv()
            dep_copy(1, step).wait_recv()
            for c in range(3):
                slip_hi = recv_dep[0, step, c] - send_dep[1, step, c]
                slip_lo = send_dep[0, step, c] - recv_dep[1, step, c]
                if c == 0:
                    grad[...] = grad[...] + TH[2, step] * slip_hi
                hi = (LOCK if c == 1 else TH[0, step]) * slip_hi
                lo = (LOCK if c == 1 else TH[1, step]) * slip_lo
                for zl in range(5):
                    sh = (96, 0) if zl < 4 else (95, -1)
                    zb = zl if zl < 4 else 0
                    rh, rl = pl.ds(8 * rblk(c, 4, zl), 8), pl.ds(8 * rblk(c, 0, zl), 8)
                    F[0, rh, :] = F[0, rh, :] - jnp.where(
                        b3, roll(hi, sh[0] - 32 * zb), 0.0
                    )
                    F[0, rl, :] = F[0, rl, :] + jnp.where(
                        b0, roll(lo, sh[1] - 32 * zb), 0.0
                    )

            for yl in range(5):
                for zl in range(5):
                    im = IM[pl.ds(8 * (yl * 5 + zl), 8), :]
                    for c in range(3):
                        r = pl.ds(8 * rblk(c, yl, zl), 8)
                        now_u = S[cur, r, :]
                        S[new, r, :] = (now_u + now_u) - S[new, r, :] - im * F[0, r, :]

            @pl.when(it == STEPS)
            def _():
                send_patches()
                from_elements(1 - STEPS % 2, 1)

            def add_side(side, first):
                plane = 0 if first == 0 else 1
                for g in range(ROWS // 8):
                    r = pl.ds(64 * g + first, 8, stride=8)
                    d = pl.ds(8 * g, 8)
                    S[new, r, :] = S[new, r, :] - IMP[plane, d, :] * recv_dom[side, step, d, :]

            @pl.when(has_r)
            def _():
                dom_copy(0, step).wait_recv()
                add_side(0, 4)

            @pl.when(has_l)
            def _():
                @pl.when(step > 0)
                def _():
                    dom_copy(1, step).wait_recv()

                add_side(1, 0)

        return carry

    lax.fori_loop(0, STEPS + 1, turn, 0)

    from_elements(STEPS % 2, 0)
    for i, off in enumerate(OFFSETS):

        @pl.when(inside(me - off))
        def _(i=i):
            patch_copy(i).wait_recv()
            out_patch[0] = out_patch[0] + precv[i, pl.ds(0, 2), :]

    @pl.when(has_l)
    def _():
        for cp in to_left:
            cp.wait_send()
        for s in range(STEPS):
            dom_copy(0, s).wait_send()

    @pl.when(has_r)
    def _():
        for cp in to_right:
            cp.wait_send()
        for s in range(1, STEPS):
            dom_copy(1, s).wait_send()

    for cp in to_up:
        cp.wait_send()
    for s in range(STEPS):
        dep_copy(0, s).wait_send()
        dep_copy(1, s).wait_send()
    for i, off in enumerate(OFFSETS):

        @pl.when(inside(me + off))
        def _(i=i):
            patch_copy(i).wait_send()


def store_results(cur, fol, patch, out_cur, out_fol, out_patch, sem):
    pairs = ((cur, out_cur), (fol, out_fol), (patch, out_patch))
    copies = [pltpu.make_async_copy(a, b, sem.at[i]) for i, (a, b) in enumerate(pairs)]
    for cp in copies:
        cp.start()
    for cp in copies:
        cp.wait()


def solution(mesh):
    nd, ndp = mesh.shape["dom"], mesh.shape["depth"]

    def on_device(now, nxt, lam, mu, dens, flags, slope, ns, owner):
        any_ = pl.BlockSpec(memory_space=pl.ANY)
        dma = pltpu.SemaphoreType.DMA
        vm = pltpu.VMEM
        i32 = jnp.int32
        cur, fol, patch = pl.pallas_call(
            functools.partial(kernel, nd, ndp),
            name="rupture",
            out_shape=(
                vm((3, 17, 4, 128), f32),
                vm((3, 17, 4, 128), f32),
                vm((1, 2, 128), f32),
            ),
            in_specs=[any_] * 9,
            out_specs=[pl.BlockSpec(memory_space=pltpu.VMEM)] * 3,
            scratch_shapes=[
                vm((2, 3, 17, 8, 128), f32),
                vm((3, 17, 8, 128), f32),
                vm((17, 8, 128), f32),
                vm((2, 2, 1, 4, 32), f32),
                vm((4, 1, 4, 128), i32),
                vm((1, 4, 128), f32),
                vm((1, 4, 128), f32),
                pltpu.SMEM((1, 4), i32),
                vm((3, 4, 1, 4, 128), i32),
                vm((3, 1, 4, 128), f32),
                vm((3, ROWS * 8, 128), f32),
                vm((2, ROWS * 8, 128), f32),
                vm((ROWS * 8, 128), f32),
                vm((ROWS * 8, 128), f32),
                vm((ROWS * 8, 128), f32),
                vm((25 * 8, 128), f32),
                vm((2, ROWS, 128), f32),
                vm((34, 8, 128), f32),
                vm((3, STEPS, 8, 128), f32),
                vm((8, 128), f32),
                vm((2, STEPS, ROWS, 128), f32),
                vm((2, STEPS, ROWS, 128), f32),
                vm((2, STEPS, 3, 8, 128), f32),
                vm((2, STEPS, 3, 8, 128), f32),
                vm((4, 8, 128), f32),
                vm((4, 8, 128), f32),
                dma((10,)),
                dma((12,)),
                dma((12,)),
                dma((2, STEPS)),
                dma((2, STEPS)),
                dma((2, STEPS)),
                dma((2, STEPS)),
                dma((4,)),
                dma((4,)),
            ],
            compiler_params=pltpu.CompilerParams(collective_id=0, has_side_effects=True),
        )(
            jnp.transpose(now, (0, 2, 1, 3)),
            jnp.transpose(nxt, (0, 2, 1, 3)),
            lam,
            mu,
            jnp.transpose(dens, (1, 0, 2)),
            flags,
            slope,
            ns,
            owner,
        )
        cur, fol, patch = pl.pallas_call(
            store_results,
            name="store_results",
            out_shape=(
                jax.ShapeDtypeStruct((3, 17, 4, 128), f32),
                jax.ShapeDtypeStruct((3, 17, 4, 128), f32),
                jax.ShapeDtypeStruct((1, 2, 128), f32),
            ),
            in_specs=[pl.BlockSpec(memory_space=pltpu.VMEM)] * 3,
            out_specs=[any_] * 3,
            scratch_shapes=[dma((3,))],
        )(*[pltpu.with_memory_space_constraint(v, pltpu.VMEM) for v in (cur, fol, patch)])
        return jnp.transpose(cur, (0, 2, 1, 3)), jnp.transpose(fol, (0, 2, 1, 3)), patch

    return jax.shard_map(
        on_device,
        mesh=mesh,
        in_specs=(
            P(None, "dom", "depth", None),
            P(None, "dom", "depth", None),
            P("dom", "depth", None),
            P("dom", "depth", None),
            P("dom", "depth", None),
            P(None, "depth", "dom", None),
            P("depth", "dom", None),
            P("depth", "dom", None),
            P("depth", "dom"),
        ),
        out_specs=(
            P(None, "dom", "depth", None),
            P(None, "dom", "depth", None),
            P("depth", "dom", None),
        ),
        check_vma=False,
    )
```

```python
import functools
import math

import jax
import jax.numpy as jnp
import numpy as np
from jax import lax
from jax.experimental import pallas as pl
from jax.experimental.pallas import tpu as pltpu
from jax.sharding import PartitionSpec as P


MESH = pl.DeviceIdType.MESH
STEPS = 4
ROWS = 80
DT2 = 0.01 * 0.01
LOCK = 0.5
W5 = [0.1, 49.0 / 90.0, 32.0 / 45.0, 49.0 / 90.0, 0.1]
OFFSETS = (-2, -1, 1, 2)
f32 = jnp.float32


def slopes5():
    pts = [-1.0, -math.sqrt(3.0 / 7.0), 0.0, math.sqrt(3.0 / 7.0), 1.0]
    prod = [np.prod([pts[a] - pts[b] for b in range(5) if b != a]) for a in range(5)]
    d = np.zeros((5, 5))
    for a in range(5):
        for b in range(5):
            if a == b:
                d[a, b] = sum(1.0 / (pts[a] - pts[o]) for o in range(5) if o != a)
            else:
                d[a, b] = prod[a] / prod[b] / (pts[a] - pts[b])
    d[2, 2] = 0.0
    return 2.0 * d


D5 = slopes5()


def apply5(m, v):
    e0, e1, o0, o1 = v[0] + v[4], v[1] + v[3], v[0] - v[4], v[1] - v[3]
    out = [None] * 5
    for q in (0, 1):
        a = (
            float((m[q, 0] + m[q, 4]) / 2) * e0
            + float((m[q, 1] + m[q, 3]) / 2) * e1
            + float(m[q, 2]) * v[2]
        )
        b = float((m[q, 0] - m[q, 4]) / 2) * o0 + float((m[q, 1] - m[q, 3]) / 2) * o1
        out[q] = b + a
        out[4 - q] = b - a
    out[2] = float((m[2, 0] - m[2, 4]) / 2) * o0 + float((m[2, 1] - m[2, 3]) / 2) * o1
    return out


def wkey(a, b):
    a, b = min(a, 4 - a), min(b, 4 - b)
    a, b = min(a, b), max(a, b)
    return {(0, 0): 0, (0, 1): 1, (0, 2): 2, (1, 1): 3, (1, 2): 4, (2, 2): 5}[(a, b)]


WPAIR = [(0, 0), (0, 1), (0, 2), (1, 1), (1, 2), (2, 2)]


def rblk(c, yl, zl):
    return (c * 5 + yl) * 5 + zl


def kernel(
    nd,
    ndp,
    now,
    nxt,
    lam,
    mu,
    dens,
    flags,
    slope,
    ns,
    owner,
    out_cur,
    out_fol,
    out_patch,
    nowv,
    nxtv,
    densv,
    modv,
    flagv,
    slopev,
    nsv,
    ownv,
    gflag,
    gslope,
    gnow,
    gnxt,
    gdens,
    GS,
    DE,
    S,
    F,
    GY,
    FX,
    FY,
    IM,
    IMP,
    CONST,
    TH,
    grad,
    send_dom,
    recv_dom,
    send_dep,
    recv_dep,
    psend,
    precv,
    lsem,
    isend,
    irecv,
    dsend,
    drecv,
    fsend,
    frecv,
    pss,
    prs,
    far,
):
    me = lax.axis_index("dom")
    my = lax.axis_index("depth")
    up = lax.rem(my + 1, ndp)
    dn = lax.rem(my + ndp - 1, ndp)
    has_l = me > 0
    has_r = me < nd - 1
    odd = lax.rem(me, 2) == 1

    barrier = pltpu.get_barrier_semaphore()
    count = 2
    for off, row in ((1, my), (-1, my), (-1, up), (1, dn)):
        ok = jnp.logical_and(me + off >= 0, me + off < nd)
        count = count + ok.astype(jnp.int32)

        @pl.when(ok)
        def _(off=off, row=row):
            pl.semaphore_signal(
                barrier, inc=1, device_id=(me + off, row), device_id_type=MESH
            )

    pl.semaphore_signal(barrier, inc=1, device_id=(me, up), device_id_type=MESH)
    pl.semaphore_signal(barrier, inc=1, device_id=(me, dn), device_id_type=MESH)

    locals_ = [
        pltpu.make_async_copy(a, b, lsem.at[i])
        for i, (a, b) in enumerate(
            [
                (now, nowv.at[0, :, :, 0:4, :]),
                (now.at[:, :, 0:1, :], nowv.at[1, :, :, 4:5, :]),
                (lam, modv.at[0, 0]),
                (mu, modv.at[0, 1]),
                (nxt, nxtv.at[:, :, 0:4, :]),
                (dens, densv.at[:, 0:4, :]),
                (flags, flagv),
                (slope, slopev),
                (ns, nsv),
                (owner, ownv),
            ]
        )
    ]
    for cp in locals_:
        cp.start()
    for cp in locals_[:6]:
        cp.wait()
    pl.semaphore_wait(barrier, count)

    def remote(i, src, dst, to):
        return pltpu.make_async_remote_copy(
            src_ref=src,
            dst_ref=dst,
            send_sem=isend.at[i],
            recv_sem=irecv.at[i],
            device_id=to,
            device_id_type=MESH,
        )

    to_left = [
        remote(0, nowv.at[0, :, :, 0, :], gnow.at[:, 0:17, :], (me - 1, my)),
        remote(1, nxtv.at[:, :, 0, :], gnxt.at[:, 0:17, :], (me - 1, my)),
        remote(2, densv.at[:, 0, :], gdens.at[0, 0:17, :], (me - 1, my)),
        remote(3, flags, gflag.at[0], (me - 1, my)),
        remote(4, slope, gslope.at[0], (me - 1, my)),
        remote(5, flags, gflag.at[1], (me - 1, up)),
        remote(6, slope, gslope.at[1], (me - 1, up)),
    ]
    to_up = [
        remote(7, flags, gflag.at[2], (me, up)),
        remote(8, slope, gslope.at[2], (me, up)),
    ]
    to_right = [
        remote(9, nowv.at[0, :, :, 0:4, :], nowv.at[1, :, :, 0:4, :], (me + 1, my)),
        remote(10, lam, modv.at[1, 0], (me + 1, my)),
        remote(11, mu, modv.at[1, 1], (me + 1, my)),
    ]

    @pl.when(has_l)
    def _():
        to_left[0].start()

    @pl.when(has_r)
    def _():
        for cp in to_right:
            cp.start()

    @pl.when(has_l)
    def _():
        for cp in to_left[1:]:
            cp.start()

    for cp in to_up:
        cp.start()

    @pl.when(jnp.logical_and(has_l, has_r))
    def _():
        pl.semaphore_signal(far.at[0], inc=1, device_id=(me - 1, my), device_id_type=MESH)
        pl.semaphore_signal(far.at[1], inc=1, device_id=(me + 1, my), device_id_type=MESH)

    lane = lax.broadcasted_iota(jnp.int32, (8, 128), 1)
    sub = lax.broadcasted_iota(jnp.int32, (8, 128), 0)
    blk = lane // 32
    ez = lane % 32
    to_packed = 4 * ez + blk
    to_natural = (lane % 4) * 32 + lane // 4
    b0, b1, b2, b3 = blk == 0, blk == 1, blk == 2, blk == 3

    def permute(x, idx):
        return jnp.take_along_axis(x, idx, axis=1)

    def roll(x, shift):
        shift = shift % 128
        return x if shift == 0 else pltpu.roll(x, shift, 1)

    def by_sub(vals):
        v = jnp.full((8, 128), 0.0, f32)
        for i, x in enumerate(vals):
            if x != 0.0:
                v = jnp.where(sub == i, float(x), v)
        return v

    for k in range(5):
        CONST[k] = by_sub(D5[:, k])
        CONST[5 + k] = by_sub(D5[k, :])

    for i in range(75, ROWS):
        for slot in range(2):
            F[slot, pl.ds(8 * i, 8), :] = jnp.zeros((8, 128), f32)
            S[slot, pl.ds(8 * i, 8), :] = jnp.zeros((8, 128), f32)

    live_x = jnp.logical_or(sub < 4, jnp.logical_and(sub == 4, has_r))

    def pick(r0, r1, r2, r3):
        return jnp.where(b0, r0, jnp.where(b1, r1, jnp.where(b2, r2, r3)))

    def to_elements(load, put, bottom):
        packed = [permute(load(y), to_packed) for y in range(17)]
        rolled = [[roll(v, 32 * s) for s in range(4)] for v in packed]
        for yl in range(5):
            for zl in range(4):
                v = pick(*[rolled[4 * e + yl][(e - zl) % 4] for e in range(4)])
                put(yl, zl, v)
                if zl == 0:
                    first = v
            put(yl, 4, jnp.where(ez == 31, bottom, roll(first, -1)))

    def wide(slot, which):
        z = jnp.zeros((1, 96), f32)
        out = jnp.zeros((8, 128), f32)
        for e in range(4):
            row = jnp.concatenate([modv[slot, which, 0, pl.ds(e, 1), :], z], axis=1)
            row = jnp.broadcast_to(row, (8, 128))
            out = jnp.where(blk == e, roll(row, 32 * e), out)
        return out

    def put_moduli(slot):
        wq = by_sub([w / 8.0 for w in W5])
        for j in range(2):
            m = wide(slot, j) * wq
            for i, (a, b) in enumerate(WPAIR):
                CONST[10 + 12 * slot + 6 * j + i] = m * float(W5[a] * W5[b])

    def mass_table():
        wx = by_sub([0.2, W5[1], W5[2], W5[3], 0.2])
        wx = jnp.where(sub == 0, jnp.where(has_l, 0.2, 0.1), wx)

        def put_mass(yl, zl, v):
            if yl in (1, 2, 3):
                wy = W5[yl]
            else:
                wy = jnp.where(b0 if yl == 0 else b3, 0.1, 0.2)
            if zl in (1, 2, 3):
                wz = W5[zl]
            elif zl == 0:
                wz = jnp.where(ez == 0, 0.1, 0.2)
            else:
                wz = 0.2
            mass = v * wx * wy * wz
            live = jnp.logical_and(live_x, ez < 31) if zl == 4 else live_x
            IM[pl.ds(8 * (yl * 5 + zl), 8), :] = jnp.where(
                live, (8.0 * DT2) / jnp.where(live, mass, 1.0), 0.0
            )

        for yl in range(5):
            for zl in range(5):
                put_mass(yl, zl, DE[pl.ds(8 * (yl * 5 + zl), 8), :])
        for plane, x in ((0, 0), (1, 4)):
            for g in range(4):
                n = 8 if g < 3 else 1
                v = IM[pl.ds(64 * g + x, n, stride=8), :] if n > 1 else IM[pl.ds(64 * g + x, 1), :]
                for c in range(3):
                    IMP[plane, pl.ds(25 * c + 8 * g, n), :] = v
            IMP[plane, pl.ds(75, 5), :] = jnp.zeros((5, 128), f32)

    def own_rows(load, outside, put):
        to_elements(lambda y: jnp.where(sub < 4, load(y), outside), put, outside)

    def own_fields():
        for slot in range(2):
            for c in range(3):

                def put(yl, zl, v, slot=slot, c=c):
                    S[slot, pl.ds(8 * rblk(c, yl, zl), 8), :] = v

                if slot == 0:
                    own_rows(lambda y, c=c: nowv[0, c, y], 0.0, put)
                else:
                    own_rows(lambda y, c=c: nxtv[c, y], 0.0, put)

        def put_dens(yl, zl, v):
            DE[pl.ds(8 * (yl * 5 + zl), 8), :] = v

        own_rows(lambda y: densv[y], 1.0, put_dens)

    def ghost_plane(ref, comps, bottom, put):
        for c in range(comps):
            for g in range(3):
                v = permute(ref[c, pl.ds(8 * g, 8), :], to_packed)
                for k in range(4):
                    GS[c, k, pl.ds(8 * g, 8), :] = roll(v, 32 * k)
        for c in range(comps):
            for zl in range(4):
                v = pick(*[GS[c, (e - zl) % 4, pl.ds(4 * e, 8), :] for e in range(4)])
                put(c, zl, v[0:5])
                if zl == 0:
                    put(c, 4, jnp.where(ez == 31, bottom, roll(v, -1))[0:5])

    def put_ghost(slot):
        def put(c, zl, v):
            S[slot, pl.ds(8 * rblk(c, 0, zl) + 4, 5, stride=40), :] = v

        return put

    def put_ghost_dens(c, zl, v):
        DE[pl.ds(8 * zl + 4, 5, stride=40), :] = v

    def fault_tables():
        def planes(own, ghost):
            top = jnp.concatenate([own, jnp.zeros((4, 128), own.dtype)], axis=0)
            low = jnp.concatenate([ghost, ghost], axis=0)
            return jnp.where(sub == 4, low, top)

        def spread(ghost):
            return jnp.broadcast_to(ghost[0:1], (4, 128))

        own_s = planes(slopev[0], spread(gslope[0, 0]))
        low_s = planes(gslope[2, 0], spread(gslope[1, 0]))
        stress = jnp.concatenate([nsv[0], jnp.zeros((4, 128), f32)], axis=0)
        for i in range(STEPS):
            own_f = planes(flagv[i, 0], spread(gflag[0, i, 0]))
            low_f = planes(gflag[2, i, 0], spread(gflag[1, i, 0]))
            for j, (fl, sl) in enumerate(((own_f, own_s), (low_f, low_s))):
                t = jnp.where(fl == 0, LOCK, jnp.where(fl == 1, -sl, 0.0))
                TH[j, i] = permute(jnp.where(live_x, t, 0.0), to_packed)
            h = jnp.where(own_f == 1, 0.5, jnp.where(own_f == 2, 1.0, 0.0))
            TH[2, i] = permute(jnp.where(sub < 4, h * stress, 0.0), to_packed)

    def dom_copy(side, step):
        to = me - 1 if side == 0 else me + 1
        return pltpu.make_async_remote_copy(
            src_ref=send_dom.at[side, step],
            dst_ref=recv_dom.at[side, step],
            send_sem=dsend.at[side, step],
            recv_sem=drecv.at[side, step],
            device_id=(to, my),
            device_id_type=MESH,
        )

    def dep_copy(side, step):
        to = dn if side == 0 else up
        return pltpu.make_async_remote_copy(
            src_ref=send_dep.at[side, step],
            dst_ref=recv_dep.at[side, step],
            send_sem=fsend.at[side, step],
            recv_sem=frecv.at[side, step],
            device_id=(me, to),
            device_id_type=MESH,
        )

    def patch_copy(i):
        return pltpu.make_async_remote_copy(
            src_ref=psend.at[i],
            dst_ref=precv.at[i],
            send_sem=pss.at[i],
            recv_sem=prs.at[i],
            device_id=(me + OFFSETS[i], my),
            device_id_type=MESH,
        )

    def inside(v):
        return jnp.logical_and(v >= 0, v < nd)

    def send_patches():
        total = permute(grad[...], to_natural)
        rows = [total[x : x + 1] for x in range(4)]

        def members(off, p):
            num = (me + off) * 2 + p
            acc = jnp.zeros((1, 128), f32)
            for x in range(4):
                acc = acc + jnp.where(ownv[0, x] == num, rows[x], 0.0)
            return acc

        for i, off in enumerate(OFFSETS):
            psend[i] = jnp.zeros((8, 128), f32)
            for p in range(2):
                psend[i, pl.ds(p, 1), :] = members(off, p)

            @pl.when(inside(me + off))
            def _(i=i):
                patch_copy(i).start()

        out_patch[0, pl.ds(0, 1), :] = members(0, 0)
        out_patch[0, pl.ds(1, 1), :] = members(0, 1)

    outs = (out_cur, out_fol)

    def from_elements(slot, which):
        for c in range(3):

            def e(yl, zl):
                return S[slot, pl.ds(8 * rblk(c, yl, zl), 8), :]

            for y in range(17):
                ey, yl = (y // 4, y % 4) if y < 16 else (3, 4)
                v = pick(*[roll(e(yl, zl), 32 * (zl - ey)) for zl in range(4)])
                outs[which][c, y] = permute(v, to_natural)[0:4]

    grad[...] = jnp.zeros((8, 128), f32)
    put_moduli(0)
    own_fields()

    def turn(it, carry):
        step = jnp.maximum(it - 1, 0)
        is_left = jnp.logical_or(
            jnp.logical_and(it == 0, odd),
            jnp.logical_and(it == 1, jnp.logical_not(odd)),
        )
        own = jnp.logical_not(is_left)
        cur = lax.rem(step, 2)
        new = 1 - cur
        fs = is_left.astype(jnp.int32)
        src = cur + 2 * fs
        cb = 10 + 12 * fs

        @pl.when(is_left)
        def _():
            @pl.when(has_l)
            def _():
                for cp in to_right:
                    cp.wait_recv()

            put_moduli(1)
            for c in range(3):

                def put(yl, zl, v, c=c):
                    S[2, pl.ds(8 * rblk(c, yl, zl), 8), :] = v

                to_elements(lambda y, c=c: jnp.where(sub < 5, nowv[1, c, y], 0.0), put, 0.0)

        @pl.when(jnp.logical_and(jnp.logical_and(own, it < 2), has_r))
        def _():
            to_left[0].wait_recv()
            ghost_plane(gnow, 3, 0.0, put_ghost(0))

        def u(c, yl, zl):
            return S[src, pl.ds(8 * rblk(c, yl, zl), 8), :]

        @pl.when(own)
        def _():
            for c in range(3):
                low = [roll(u(c, 0, z), 32 * z) for z in range(4)]
                high = [roll(u(c, 4, z), 32 * (z - 3)) for z in range(4)]
                send_dep[0, step, c] = pick(*low)
                send_dep[1, step, c] = pick(*high)
            dep_copy(0, step).start()
            dep_copy(1, step).start()

        for c in range(3):
            for zl in range(5):
                g = apply5(D5, [u(c, yl, zl) for yl in range(5)])
                for yl in range(5):
                    GY[pl.ds(8 * rblk(c, yl, zl), 8), :] = g[yl]
        for yl in range(5):
            gz = [apply5(D5, [u(c, yl, zl) for zl in range(5)]) for c in range(3)]
            fz = [[None] * 5 for _ in range(3)]
            for zl in range(5):
                gx, gy = [], []
                for c in range(3):
                    r = 8 * rblk(c, yl, zl)
                    acc = None
                    for k in range(5):
                        row = jnp.broadcast_to(S[src, pl.ds(r + k, 1), :], (8, 128))
                        t = row * CONST[k]
                        acc = t if acc is None else acc + t
                    gx.append(acc)
                    gy.append(GY[pl.ds(r, 8), :])
                key = wkey(yl, zl)
                lw, mw = CONST[cb + key], CONST[cb + 6 + key]
                m2 = mw + mw
                common = lw * (gx[0] + gy[1] + gz[2][zl])
                sxx = common + m2 * gx[0]
                syy = common + m2 * gy[1]
                szz = common + m2 * gz[2][zl]
                sxy = mw * (gx[1] + gy[0])
                sxz = mw * (gx[2] + gz[0][zl])
                syz = mw * (gy[2] + gz[1][zl])
                for c, (vx, vy, vz) in enumerate(
                    ((sxx, sxy, sxz), (sxy, syy, syz), (sxz, syz, szz))
                ):
                    r = 8 * rblk(c, yl, zl)
                    FX[pl.ds(r, 8), :] = vx
                    FY[pl.ds(r, 8), :] = vy
                    fz[c][zl] = vz
            for c in range(3):
                back = apply5(D5.T, fz[c])
                for zl in range(5):
                    F[fs, pl.ds(8 * rblk(c, yl, zl), 8), :] = back[zl]
        for c in range(3):
            for zl in range(5):
                rs = [8 * rblk(c, yl, zl) for yl in range(5)]
                back = apply5(D5.T, [FY[pl.ds(r, 8), :] for r in rs])
                for yl, r in enumerate(rs):
                    acc = back[yl] + F[fs, pl.ds(r, 8), :]
                    for q in range(5):
                        row = jnp.broadcast_to(FX[pl.ds(r + q, 1), :], (8, 128))
                        acc = acc + row * CONST[5 + q]
                    F[fs, pl.ds(r, 8), :] = acc

        for c in range(3):
            for yl in range(5):
                ra, rb = pl.ds(8 * rblk(c, yl, 0), 8), pl.ds(8 * rblk(c, yl, 4), 8)
                fa, fb = F[fs, ra, :], F[fs, rb, :]
                F[fs, ra, :] = fa + jnp.where(ez == 0, 0.0, roll(fb, 1))
                F[fs, rb, :] = fb + roll(fa, -1)
        for c in range(3):
            for zl in range(5):
                ra, rb = pl.ds(8 * rblk(c, 0, zl), 8), pl.ds(8 * rblk(c, 4, zl), 8)
                fa, fb = F[fs, ra, :], F[fs, rb, :]
                F[fs, ra, :] = fa + jnp.where(b0, 0.0, roll(fb, 32))
                F[fs, rb, :] = fb + jnp.where(b3, 0.0, roll(fa, -32))

        @pl.when(is_left)
        def _():
            for g in range(ROWS // 8):
                recv_dom[1, 0, pl.ds(8 * g, 8), :] = F[1, pl.ds(64 * g + 4, 8, stride=8), :]

        @pl.when(own)
        def _():
            for g in range(ROWS // 8):
                d = pl.ds(8 * g, 8)
                send_dom[0, step, d, :] = F[0, pl.ds(64 * g, 8, stride=8), :]
                send_dom[1, step, d, :] = F[0, pl.ds(64 * g + 4, 8, stride=8), :]

            @pl.when(has_l)
            def _():
                dom_copy(0, step).start()

            @pl.when(jnp.logical_and(has_r, step > 0))
            def _():
                dom_copy(1, step).start()

        @pl.when(it == odd.astype(jnp.int32))
        def _():
            for cp in locals_[6:]:
                cp.wait()
            for cp in to_up:
                cp.wait_recv()

            @pl.when(has_r)
            def _():
                for cp in to_left[1:]:
                    cp.wait_recv()
                ghost_plane(gnxt, 3, 0.0, put_ghost(1))
                ghost_plane(gdens, 1, 1.0, put_ghost_dens)

            mass_table()
            fault_tables()

        @pl.when(it > 0)
        def _():
            dep_copy(0, step).wait_recv()
            dep_copy(1, step).wait_recv()
            for c in range(3):
                slip_hi = recv_dep[0, step, c] - send_dep[1, step, c]
                slip_lo = send_dep[0, step, c] - recv_dep[1, step, c]
                if c == 0:
                    grad[...] = grad[...] + TH[2, step] * slip_hi
                hi = (LOCK if c == 1 else TH[0, step]) * slip_hi
                lo = (LOCK if c == 1 else TH[1, step]) * slip_lo
                rh = [pl.ds(8 * rblk(c, 4, zl), 8) for zl in range(5)]
                rl = [pl.ds(8 * rblk(c, 0, zl), 8) for zl in range(5)]
                vh, vl = [], []
                for zl in range(5):
                    sh = (96, 0) if zl < 4 else (95, -1)
                    zb = zl if zl < 4 else 0
                    vh.append(
                        F[0, rh[zl], :] - jnp.where(b3, roll(hi, sh[0] - 32 * zb), 0.0)
                    )
                    vl.append(
                        F[0, rl[zl], :] + jnp.where(b0, roll(lo, sh[1] - 32 * zb), 0.0)
                    )
                for zl in range(5):
                    F[0, rh[zl], :] = vh[zl]
                    F[0, rl[zl], :] = vl[zl]

            for yl in range(5):
                rs = [pl.ds(8 * rblk(c, yl, zl), 8) for zl in range(5) for c in range(3)]
                ims = [IM[pl.ds(8 * (yl * 5 + zl), 8), :] for zl in range(5)]
                news = []
                for i, r in enumerate(rs):
                    now_u = S[cur, r, :]
                    news.append((now_u + now_u) - S[new, r, :] - ims[i // 3] * F[0, r, :])
                for r, v in zip(rs, news):
                    S[new, r, :] = v

            @pl.when(it == STEPS)
            def _():
                @pl.when(me + 2 < nd)
                def _():
                    pl.semaphore_wait(far.at[0], 1)

                @pl.when(me - 2 >= 0)
                def _():
                    pl.semaphore_wait(far.at[1], 1)

                send_patches()
                from_elements(1 - STEPS % 2, 1)

            def add_side(side, first):
                plane = 0 if first == 0 else 1
                rs = [pl.ds(64 * g + first, 8, stride=8) for g in range(ROWS // 8)]
                ds = [pl.ds(8 * g, 8) for g in range(ROWS // 8)]
                news = [
                    S[new, r, :] - IMP[plane, d, :] * recv_dom[side, step, d, :]
                    for r, d in zip(rs, ds)
                ]
                for r, v in zip(rs, news):
                    S[new, r, :] = v

            @pl.when(has_r)
            def _():
                dom_copy(0, step).wait_recv()
                add_side(0, 4)

            @pl.when(has_l)
            def _():
                @pl.when(step > 0)
                def _():
                    dom_copy(1, step).wait_recv()

                add_side(1, 0)

        return carry

    lax.fori_loop(0, STEPS + 1, turn, 0)

    from_elements(STEPS % 2, 0)
    for i, off in enumerate(OFFSETS):

        @pl.when(inside(me - off))
        def _(i=i):
            patch_copy(i).wait_recv()
            out_patch[0] = out_patch[0] + precv[i, pl.ds(0, 2), :]

    @pl.when(has_l)
    def _():
        for cp in to_left:
            cp.wait_send()
        for s in range(STEPS):
            dom_copy(0, s).wait_send()

    @pl.when(has_r)
    def _():
        for cp in to_right:
            cp.wait_send()
        for s in range(1, STEPS):
            dom_copy(1, s).wait_send()

    for cp in to_up:
        cp.wait_send()
    for s in range(STEPS):
        dep_copy(0, s).wait_send()
        dep_copy(1, s).wait_send()
    for i, off in enumerate(OFFSETS):

        @pl.when(inside(me + off))
        def _(i=i):
            patch_copy(i).wait_send()


def store_results(cur, fol, patch, out_cur, out_fol, out_patch, sem):
    pairs = ((cur, out_cur), (fol, out_fol), (patch, out_patch))
    copies = [pltpu.make_async_copy(a, b, sem.at[i]) for i, (a, b) in enumerate(pairs)]
    for cp in copies:
        cp.start()
    for cp in copies:
        cp.wait()


def solution(mesh):
    nd, ndp = mesh.shape["dom"], mesh.shape["depth"]

    def on_device(now, nxt, lam, mu, dens, flags, slope, ns, owner):
        any_ = pl.BlockSpec(memory_space=pl.ANY)
        dma = pltpu.SemaphoreType.DMA
        vm = pltpu.VMEM
        i32 = jnp.int32
        cur, fol, patch = pl.pallas_call(
            functools.partial(kernel, nd, ndp),
            name="rupture",
            out_shape=(
                vm((3, 17, 4, 128), f32),
                vm((3, 17, 4, 128), f32),
                vm((1, 2, 128), f32),
            ),
            in_specs=[any_] * 9,
            out_specs=[pl.BlockSpec(memory_space=pltpu.VMEM)] * 3,
            scratch_shapes=[
                vm((2, 3, 17, 8, 128), f32),
                vm((3, 17, 8, 128), f32),
                vm((17, 8, 128), f32),
                vm((2, 2, 1, 4, 32), f32),
                vm((4, 1, 4, 128), i32),
                vm((1, 4, 128), f32),
                vm((1, 4, 128), f32),
                pltpu.SMEM((1, 4), i32),
                vm((3, 4, 1, 4, 128), i32),
                vm((3, 1, 4, 128), f32),
                vm((3, 24, 128), f32),
                vm((3, 24, 128), f32),
                vm((1, 24, 128), f32),
                vm((3, 4, 24, 128), f32),
                vm((25 * 8, 128), f32),
                vm((3, ROWS * 8, 128), f32),
                vm((2, ROWS * 8, 128), f32),
                vm((ROWS * 8, 128), f32),
                vm((ROWS * 8, 128), f32),
                vm((ROWS * 8, 128), f32),
                vm((25 * 8, 128), f32),
                vm((2, ROWS, 128), f32),
                vm((34, 8, 128), f32),
                vm((3, STEPS, 8, 128), f32),
                vm((8, 128), f32),
                vm((2, STEPS, ROWS, 128), f32),
                vm((2, STEPS, ROWS, 128), f32),
                vm((2, STEPS, 3, 8, 128), f32),
                vm((2, STEPS, 3, 8, 128), f32),
                vm((4, 8, 128), f32),
                vm((4, 8, 128), f32),
                dma((10,)),
                dma((12,)),
                dma((12,)),
                dma((2, STEPS)),
                dma((2, STEPS)),
                dma((2, STEPS)),
                dma((2, STEPS)),
                dma((4,)),
                dma((4,)),
                pltpu.SemaphoreType.REGULAR((2,)),
            ],
            compiler_params=pltpu.CompilerParams(collective_id=0, has_side_effects=True),
        )(
            jnp.transpose(now, (0, 2, 1, 3)),
            jnp.transpose(nxt, (0, 2, 1, 3)),
            lam,
            mu,
            jnp.transpose(dens, (1, 0, 2)),
            flags,
            slope,
            ns,
            owner,
        )
        cur, fol, patch = pl.pallas_call(
            store_results,
            name="store_results",
            out_shape=(
                jax.ShapeDtypeStruct((3, 17, 4, 128), f32),
                jax.ShapeDtypeStruct((3, 17, 4, 128), f32),
                jax.ShapeDtypeStruct((1, 2, 128), f32),
            ),
            in_specs=[pl.BlockSpec(memory_space=pltpu.VMEM)] * 3,
            out_specs=[any_] * 3,
            scratch_shapes=[dma((3,))],
        )(*[pltpu.with_memory_space_constraint(v, pltpu.VMEM) for v in (cur, fol, patch)])
        return jnp.transpose(cur, (0, 2, 1, 3)), jnp.transpose(fol, (0, 2, 1, 3)), patch

    return jax.shard_map(
        on_device,
        mesh=mesh,
        in_specs=(
            P(None, "dom", "depth", None),
            P(None, "dom", "depth", None),
            P("dom", "depth", None),
            P("dom", "depth", None),
            P("dom", "depth", None),
            P(None, "depth", "dom", None),
            P("depth", "dom", None),
            P("depth", "dom", None),
            P("depth", "dom"),
        ),
        out_specs=(
            P(None, "dom", "depth", None),
            P(None, "dom", "depth", None),
            P("depth", "dom", None),
        ),
        check_vma=False,
    )
```

```python
import functools
import math

import jax
import jax.numpy as jnp
import numpy as np
from jax import lax
from jax.experimental import pallas as pl
from jax.experimental.pallas import tpu as pltpu
from jax.sharding import PartitionSpec as P


MESH = pl.DeviceIdType.MESH
STEPS = 4
ROWS = 80
DT2 = 0.01 * 0.01
LOCK = 0.5
W5 = [0.1, 49.0 / 90.0, 32.0 / 45.0, 49.0 / 90.0, 0.1]
OFFSETS = (-2, -1, 1, 2)
f32 = jnp.float32


def slopes5():
    pts = [-1.0, -math.sqrt(3.0 / 7.0), 0.0, math.sqrt(3.0 / 7.0), 1.0]
    prod = [np.prod([pts[a] - pts[b] for b in range(5) if b != a]) for a in range(5)]
    d = np.zeros((5, 5))
    for a in range(5):
        for b in range(5):
            if a == b:
                d[a, b] = sum(1.0 / (pts[a] - pts[o]) for o in range(5) if o != a)
            else:
                d[a, b] = prod[a] / prod[b] / (pts[a] - pts[b])
    d[2, 2] = 0.0
    return 2.0 * d


D5 = slopes5()


def apply5(m, v):
    e0, e1, o0, o1 = v[0] + v[4], v[1] + v[3], v[0] - v[4], v[1] - v[3]
    out = [None] * 5
    for q in (0, 1):
        a = (
            float((m[q, 0] + m[q, 4]) / 2) * e0
            + float((m[q, 1] + m[q, 3]) / 2) * e1
            + float(m[q, 2]) * v[2]
        )
        b = float((m[q, 0] - m[q, 4]) / 2) * o0 + float((m[q, 1] - m[q, 3]) / 2) * o1
        out[q] = b + a
        out[4 - q] = b - a
    out[2] = float((m[2, 0] - m[2, 4]) / 2) * o0 + float((m[2, 1] - m[2, 3]) / 2) * o1
    return out


def wkey(a, b):
    a, b = min(a, 4 - a), min(b, 4 - b)
    a, b = min(a, b), max(a, b)
    return {(0, 0): 0, (0, 1): 1, (0, 2): 2, (1, 1): 3, (1, 2): 4, (2, 2): 5}[(a, b)]


WPAIR = [(0, 0), (0, 1), (0, 2), (1, 1), (1, 2), (2, 2)]


def rblk(c, yl, zl):
    return (c * 5 + yl) * 5 + zl


def kernel(
    nd,
    ndp,
    now,
    nxt,
    lam,
    mu,
    dens,
    flags,
    slope,
    ns,
    owner,
    out_cur,
    out_fol,
    out_patch,
    nowv,
    nxtv,
    densv,
    modv,
    flagv,
    slopev,
    nsv,
    ownv,
    gflag,
    gslope,
    gnow,
    gnxt,
    gdens,
    GS,
    DE,
    S,
    F,
    GY,
    FX,
    FY,
    IM,
    IMP,
    CONST,
    TH,
    grad,
    send_dom,
    recv_dom,
    send_dep,
    recv_dep,
    psend,
    precv,
    lsem,
    isend,
    irecv,
    dsend,
    drecv,
    fsend,
    frecv,
    pss,
    prs,
    far,
):
    me = lax.axis_index("dom")
    my = lax.axis_index("depth")
    up = lax.rem(my + 1, ndp)
    dn = lax.rem(my + ndp - 1, ndp)
    has_l = me > 0
    has_r = me < nd - 1
    odd = lax.rem(me, 2) == 1

    barrier = pltpu.get_barrier_semaphore()
    count = 2
    for off, row in ((1, my), (-1, my), (-1, up), (1, dn)):
        ok = jnp.logical_and(me + off >= 0, me + off < nd)
        count = count + ok.astype(jnp.int32)

        @pl.when(ok)
        def _(off=off, row=row):
            pl.semaphore_signal(
                barrier, inc=1, device_id=(me + off, row), device_id_type=MESH
            )

    pl.semaphore_signal(barrier, inc=1, device_id=(me, up), device_id_type=MESH)
    pl.semaphore_signal(barrier, inc=1, device_id=(me, dn), device_id_type=MESH)

    locals_ = [
        pltpu.make_async_copy(a, b, lsem.at[i])
        for i, (a, b) in enumerate(
            [
                (now, nowv.at[0, :, :, 0:4, :]),
                (now.at[:, :, 0:1, :], nowv.at[1, :, :, 4:5, :]),
                (lam, modv.at[0, 0]),
                (mu, modv.at[0, 1]),
                (nxt, nxtv.at[:, :, 0:4, :]),
                (dens, densv.at[:, 0:4, :]),
                (flags, flagv),
                (slope, slopev),
                (ns, nsv),
                (owner, ownv),
            ]
        )
    ]
    for cp in locals_:
        cp.start()
    for cp in locals_[:6]:
        cp.wait()
    pl.semaphore_wait(barrier, count)

    def remote(i, src, dst, to):
        return pltpu.make_async_remote_copy(
            src_ref=src,
            dst_ref=dst,
            send_sem=isend.at[i],
            recv_sem=irecv.at[i],
            device_id=to,
            device_id_type=MESH,
        )

    to_left = [
        remote(0, nowv.at[0, :, :, 0, :], gnow.at[:, 0:17, :], (me - 1, my)),
        remote(1, nxtv.at[:, :, 0, :], gnxt.at[:, 0:17, :], (me - 1, my)),
        remote(2, densv.at[:, 0, :], gdens.at[0, 0:17, :], (me - 1, my)),
        remote(3, flags, gflag.at[0], (me - 1, my)),
        remote(4, slope, gslope.at[0], (me - 1, my)),
        remote(5, flags, gflag.at[1], (me - 1, up)),
        remote(6, slope, gslope.at[1], (me - 1, up)),
    ]
    to_up = [
        remote(7, flags, gflag.at[2], (me, up)),
        remote(8, slope, gslope.at[2], (me, up)),
    ]
    to_right = [
        remote(9, nowv.at[0, :, :, 0:4, :], nowv.at[1, :, :, 0:4, :], (me + 1, my)),
        remote(10, lam, modv.at[1, 0], (me + 1, my)),
        remote(11, mu, modv.at[1, 1], (me + 1, my)),
    ]

    @pl.when(has_l)
    def _():
        to_left[0].start()

    @pl.when(has_r)
    def _():
        for cp in to_right:
            cp.start()

    @pl.when(has_l)
    def _():
        for cp in to_left[1:]:
            cp.start()

    for cp in to_up:
        cp.start()

    @pl.when(jnp.logical_and(has_l, has_r))
    def _():
        pl.semaphore_signal(far.at[0], inc=1, device_id=(me - 1, my), device_id_type=MESH)
        pl.semaphore_signal(far.at[1], inc=1, device_id=(me + 1, my), device_id_type=MESH)

    lane = lax.broadcasted_iota(jnp.int32, (8, 128), 1)
    sub = lax.broadcasted_iota(jnp.int32, (8, 128), 0)
    blk = lane // 32
    ez = lane % 32
    to_packed = 4 * ez + blk
    to_natural = (lane % 4) * 32 + lane // 4
    b0, b1, b2, b3 = blk == 0, blk == 1, blk == 2, blk == 3

    def permute(x, idx):
        return jnp.take_along_axis(x, idx, axis=1)

    def roll(x, shift):
        shift = shift % 128
        return x if shift == 0 else pltpu.roll(x, shift, 1)

    def by_sub(vals):
        v = jnp.full((8, 128), 0.0, f32)
        for i, x in enumerate(vals):
            if x != 0.0:
                v = jnp.where(sub == i, float(x), v)
        return v

    for k in range(5):
        CONST[k] = by_sub(D5[:, k])
        CONST[5 + k] = by_sub(D5[k, :])

    for i in range(75, ROWS):
        for slot in range(2):
            F[slot, pl.ds(8 * i, 8), :] = jnp.zeros((8, 128), f32)
            S[slot, pl.ds(8 * i, 8), :] = jnp.zeros((8, 128), f32)

    live_x = jnp.logical_or(sub < 4, jnp.logical_and(sub == 4, has_r))

    def pick(r0, r1, r2, r3):
        return jnp.where(b0, r0, jnp.where(b1, r1, jnp.where(b2, r2, r3)))

    def to_elements(load, put, bottom):
        packed = [permute(load(y), to_packed) for y in range(17)]
        rolled = [[roll(v, 32 * s) for s in range(4)] for v in packed]
        for yl in range(5):
            for zl in range(4):
                v = pick(*[rolled[4 * e + yl][(e - zl) % 4] for e in range(4)])
                put(yl, zl, v)
                if zl == 0:
                    first = v
            put(yl, 4, jnp.where(ez == 31, bottom, roll(first, -1)))

    def wide(slot, which):
        z = jnp.zeros((1, 96), f32)
        out = jnp.zeros((8, 128), f32)
        for e in range(4):
            row = jnp.concatenate([modv[slot, which, 0, pl.ds(e, 1), :], z], axis=1)
            row = jnp.broadcast_to(row, (8, 128))
            out = jnp.where(blk == e, roll(row, 32 * e), out)
        return out

    def put_moduli(slot):
        wq = by_sub([w / 8.0 for w in W5])
        for j in range(2):
            m = wide(slot, j) * wq
            for i, (a, b) in enumerate(WPAIR):
                CONST[10 + 12 * slot + 6 * j + i] = m * float(W5[a] * W5[b])

    def mass_table():
        wx = by_sub([0.2, W5[1], W5[2], W5[3], 0.2])
        wx = jnp.where(sub == 0, jnp.where(has_l, 0.2, 0.1), wx)

        def put_mass(yl, zl, v):
            if yl in (1, 2, 3):
                wy = W5[yl]
            else:
                wy = jnp.where(b0 if yl == 0 else b3, 0.1, 0.2)
            if zl in (1, 2, 3):
                wz = W5[zl]
            elif zl == 0:
                wz = jnp.where(ez == 0, 0.1, 0.2)
            else:
                wz = 0.2
            mass = v * wx * wy * wz
            live = jnp.logical_and(live_x, ez < 31) if zl == 4 else live_x
            IM[pl.ds(8 * (yl * 5 + zl), 8), :] = jnp.where(
                live, (8.0 * DT2) / jnp.where(live, mass, 1.0), 0.0
            )

        for yl in range(5):
            for zl in range(5):
                put_mass(yl, zl, DE[pl.ds(8 * (yl * 5 + zl), 8), :])
        for plane, x in ((0, 0), (1, 4)):
            for g in range(4):
                n = 8 if g < 3 else 1
                v = IM[pl.ds(64 * g + x, n, stride=8), :] if n > 1 else IM[pl.ds(64 * g + x, 1), :]
                for c in range(3):
                    IMP[plane, pl.ds(25 * c + 8 * g, n), :] = v
            IMP[plane, pl.ds(75, 5), :] = jnp.zeros((5, 128), f32)

    def own_rows(load, outside, put):
        to_elements(lambda y: jnp.where(sub < 4, load(y), outside), put, outside)

    def own_fields():
        for slot in range(2):
            for c in range(3):

                def put(yl, zl, v, slot=slot, c=c):
                    S[slot, pl.ds(8 * rblk(c, yl, zl), 8), :] = v

                if slot == 0:
                    own_rows(lambda y, c=c: nowv[0, c, y], 0.0, put)
                else:
                    own_rows(lambda y, c=c: nxtv[c, y], 0.0, put)

        def put_dens(yl, zl, v):
            DE[pl.ds(8 * (yl * 5 + zl), 8), :] = v

        own_rows(lambda y: densv[y], 1.0, put_dens)

    def ghost_plane(ref, comps, bottom, put):
        for c in range(comps):
            for g in range(3):
                v = permute(ref[c, pl.ds(8 * g, 8), :], to_packed)
                for k in range(4):
                    GS[c, k, pl.ds(8 * g, 8), :] = roll(v, 32 * k)
        for c in range(comps):
            for zl in range(4):
                v = pick(*[GS[c, (e - zl) % 4, pl.ds(4 * e, 8), :] for e in range(4)])
                put(c, zl, v[0:5])
                if zl == 0:
                    put(c, 4, jnp.where(ez == 31, bottom, roll(v, -1))[0:5])

    def put_ghost(slot):
        def put(c, zl, v):
            S[slot, pl.ds(8 * rblk(c, 0, zl) + 4, 5, stride=40), :] = v

        return put

    def put_ghost_dens(c, zl, v):
        DE[pl.ds(8 * zl + 4, 5, stride=40), :] = v

    def fault_tables():
        def planes(own, ghost):
            top = jnp.concatenate([own, jnp.zeros((4, 128), own.dtype)], axis=0)
            low = jnp.concatenate([ghost, ghost], axis=0)
            return jnp.where(sub == 4, low, top)

        def spread(ghost):
            return jnp.broadcast_to(ghost[0:1], (4, 128))

        own_s = planes(slopev[0], spread(gslope[0, 0]))
        low_s = planes(gslope[2, 0], spread(gslope[1, 0]))
        stress = jnp.concatenate([nsv[0], jnp.zeros((4, 128), f32)], axis=0)
        for i in range(STEPS):
            own_f = planes(flagv[i, 0], spread(gflag[0, i, 0]))
            low_f = planes(gflag[2, i, 0], spread(gflag[1, i, 0]))
            for j, (fl, sl) in enumerate(((own_f, own_s), (low_f, low_s))):
                t = jnp.where(fl == 0, LOCK, jnp.where(fl == 1, -sl, 0.0))
                TH[j, i] = permute(jnp.where(live_x, t, 0.0), to_packed)
            h = jnp.where(own_f == 1, 0.5, jnp.where(own_f == 2, 1.0, 0.0))
            TH[2, i] = permute(jnp.where(sub < 4, h * stress, 0.0), to_packed)

    def dom_copy(side, step):
        to = me - 1 if side == 0 else me + 1
        return pltpu.make_async_remote_copy(
            src_ref=send_dom.at[side, step],
            dst_ref=recv_dom.at[side, step],
            send_sem=dsend.at[side, step],
            recv_sem=drecv.at[side, step],
            device_id=(to, my),
            device_id_type=MESH,
        )

    def dep_copy(side, step):
        to = dn if side == 0 else up
        return pltpu.make_async_remote_copy(
            src_ref=send_dep.at[side, step],
            dst_ref=recv_dep.at[side, step],
            send_sem=fsend.at[side, step],
            recv_sem=frecv.at[side, step],
            device_id=(me, to),
            device_id_type=MESH,
        )

    def patch_copy(i):
        return pltpu.make_async_remote_copy(
            src_ref=psend.at[i],
            dst_ref=precv.at[i],
            send_sem=pss.at[i],
            recv_sem=prs.at[i],
            device_id=(me + OFFSETS[i], my),
            device_id_type=MESH,
        )

    def inside(v):
        return jnp.logical_and(v >= 0, v < nd)

    def send_patches():
        total = permute(grad[...], to_natural)
        rows = [total[x : x + 1] for x in range(4)]

        def members(off, p):
            num = (me + off) * 2 + p
            acc = jnp.zeros((1, 128), f32)
            for x in range(4):
                acc = acc + jnp.where(ownv[0, x] == num, rows[x], 0.0)
            return acc

        for i, off in enumerate(OFFSETS):
            psend[i] = jnp.zeros((8, 128), f32)
            for p in range(2):
                psend[i, pl.ds(p, 1), :] = members(off, p)

            @pl.when(inside(me + off))
            def _(i=i):
                patch_copy(i).start()

        out_patch[0, pl.ds(0, 1), :] = members(0, 0)
        out_patch[0, pl.ds(1, 1), :] = members(0, 1)

    outs = (out_cur, out_fol)

    def from_elements(slot, which):
        for c in range(3):

            def e(yl, zl):
                return S[slot, pl.ds(8 * rblk(c, yl, zl), 8), :]

            for y in range(17):
                ey, yl = (y // 4, y % 4) if y < 16 else (3, 4)
                v = pick(*[roll(e(yl, zl), 32 * (zl - ey)) for zl in range(4)])
                outs[which][c, y] = permute(v, to_natural)[0:4]

    grad[...] = jnp.zeros((8, 128), f32)
    put_moduli(0)
    own_fields()

    def turn(it, carry):
        step = jnp.maximum(it - 1, 0)
        is_left = jnp.logical_or(
            jnp.logical_and(it == 0, odd),
            jnp.logical_and(it == 1, jnp.logical_not(odd)),
        )
        own = jnp.logical_not(is_left)
        cur = lax.rem(step, 2)
        new = 1 - cur
        fs = is_left.astype(jnp.int32)
        src = cur + 2 * fs
        cb = 10 + 12 * fs

        @pl.when(is_left)
        def _():
            @pl.when(has_l)
            def _():
                for cp in to_right:
                    cp.wait_recv()

            put_moduli(1)
            for c in range(3):

                def put(yl, zl, v, c=c):
                    S[2, pl.ds(8 * rblk(c, yl, zl), 8), :] = v

                to_elements(lambda y, c=c: jnp.where(sub < 5, nowv[1, c, y], 0.0), put, 0.0)

        @pl.when(jnp.logical_and(jnp.logical_and(own, it < 2), has_r))
        def _():
            to_left[0].wait_recv()
            ghost_plane(gnow, 3, 0.0, put_ghost(0))

        def u(c, yl, zl):
            return S[src, pl.ds(8 * rblk(c, yl, zl), 8), :]

        @pl.when(own)
        def _():
            for c in range(3):
                low = [roll(u(c, 0, z), 32 * z) for z in range(4)]
                high = [roll(u(c, 4, z), 32 * (z - 3)) for z in range(4)]
                send_dep[0, step, c] = pick(*low)
                send_dep[1, step, c] = pick(*high)
            dep_copy(0, step).start()
            dep_copy(1, step).start()

        for c in range(3):
            for zl in range(5):
                g = apply5(D5, [u(c, yl, zl) for yl in range(5)])
                for yl in range(5):
                    GY[pl.ds(8 * rblk(c, yl, zl), 8), :] = g[yl]
        for yl in range(5):
            gz = [apply5(D5, [u(c, yl, zl) for zl in range(5)]) for c in range(3)]
            fz = [[None] * 5 for _ in range(3)]
            for zl in range(5):
                gx, gy = [], []
                for c in range(3):
                    r = 8 * rblk(c, yl, zl)
                    acc = None
                    for k in range(5):
                        row = jnp.broadcast_to(S[src, pl.ds(r + k, 1), :], (8, 128))
                        t = row * CONST[k]
                        acc = t if acc is None else acc + t
                    gx.append(acc)
                    gy.append(GY[pl.ds(r, 8), :])
                key = wkey(yl, zl)
                lw, mw = CONST[cb + key], CONST[cb + 6 + key]
                m2 = mw + mw
                common = lw * (gx[0] + gy[1] + gz[2][zl])
                sxx = common + m2 * gx[0]
                syy = common + m2 * gy[1]
                szz = common + m2 * gz[2][zl]
                sxy = mw * (gx[1] + gy[0])
                sxz = mw * (gx[2] + gz[0][zl])
                syz = mw * (gy[2] + gz[1][zl])
                for c, (vx, vy, vz) in enumerate(
                    ((sxx, sxy, sxz), (sxy, syy, syz), (sxz, syz, szz))
                ):
                    r = 8 * rblk(c, yl, zl)
                    FX[pl.ds(r, 8), :] = vx
                    FY[pl.ds(r, 8), :] = vy
                    fz[c][zl] = vz
            for c in range(3):
                back = apply5(D5.T, fz[c])
                for zl in range(5):
                    F[fs, pl.ds(8 * rblk(c, yl, zl), 8), :] = back[zl]
        for c in range(3):
            for zl in range(5):
                rs = [8 * rblk(c, yl, zl) for yl in range(5)]
                back = apply5(D5.T, [FY[pl.ds(r, 8), :] for r in rs])
                for yl, r in enumerate(rs):
                    acc = back[yl] + F[fs, pl.ds(r, 8), :]
                    for q in range(5):
                        row = jnp.broadcast_to(FX[pl.ds(r + q, 1), :], (8, 128))
                        acc = acc + row * CONST[5 + q]
                    F[fs, pl.ds(r, 8), :] = acc

        for c in range(3):
            for yl in range(5):
                ra, rb = pl.ds(8 * rblk(c, yl, 0), 8), pl.ds(8 * rblk(c, yl, 4), 8)
                fa, fb = F[fs, ra, :], F[fs, rb, :]
                F[fs, ra, :] = fa + jnp.where(ez == 0, 0.0, roll(fb, 1))
                F[fs, rb, :] = fb + roll(fa, -1)
        for c in range(3):
            for zl in range(5):
                ra, rb = pl.ds(8 * rblk(c, 0, zl), 8), pl.ds(8 * rblk(c, 4, zl), 8)
                fa, fb = F[fs, ra, :], F[fs, rb, :]
                F[fs, ra, :] = fa + jnp.where(b0, 0.0, roll(fb, 32))
                F[fs, rb, :] = fb + jnp.where(b3, 0.0, roll(fa, -32))

        @pl.when(is_left)
        def _():
            for g in range(ROWS // 8):
                recv_dom[1, 0, pl.ds(8 * g, 8), :] = F[1, pl.ds(64 * g + 4, 8, stride=8), :]

        @pl.when(own)
        def _():
            for g in range(ROWS // 8):
                d = pl.ds(8 * g, 8)
                send_dom[0, step, d, :] = F[0, pl.ds(64 * g, 8, stride=8), :]
                send_dom[1, step, d, :] = F[0, pl.ds(64 * g + 4, 8, stride=8), :]

            @pl.when(jnp.logical_and(has_l, step < STEPS - 1))
            def _():
                dom_copy(0, step).start()

            @pl.when(jnp.logical_and(has_r, step > 0))
            def _():
                dom_copy(1, step).start()

        @pl.when(it == odd.astype(jnp.int32))
        def _():
            for cp in locals_[6:]:
                cp.wait()
            for cp in to_up:
                cp.wait_recv()

            @pl.when(has_r)
            def _():
                for cp in to_left[1:]:
                    cp.wait_recv()
                ghost_plane(gnxt, 3, 0.0, put_ghost(1))
                ghost_plane(gdens, 1, 1.0, put_ghost_dens)

            mass_table()
            fault_tables()

        @pl.when(it > 0)
        def _():
            dep_copy(0, step).wait_recv()
            dep_copy(1, step).wait_recv()
            for c in range(3):
                slip_hi = recv_dep[0, step, c] - send_dep[1, step, c]
                slip_lo = send_dep[0, step, c] - recv_dep[1, step, c]
                if c == 0:
                    grad[...] = grad[...] + TH[2, step] * slip_hi
                hi = (LOCK if c == 1 else TH[0, step]) * slip_hi
                lo = (LOCK if c == 1 else TH[1, step]) * slip_lo
                rh = [pl.ds(8 * rblk(c, 4, zl), 8) for zl in range(5)]
                rl = [pl.ds(8 * rblk(c, 0, zl), 8) for zl in range(5)]
                vh, vl = [], []
                for zl in range(5):
                    sh = (96, 0) if zl < 4 else (95, -1)
                    zb = zl if zl < 4 else 0
                    vh.append(
                        F[0, rh[zl], :] - jnp.where(b3, roll(hi, sh[0] - 32 * zb), 0.0)
                    )
                    vl.append(
                        F[0, rl[zl], :] + jnp.where(b0, roll(lo, sh[1] - 32 * zb), 0.0)
                    )
                for zl in range(5):
                    F[0, rh[zl], :] = vh[zl]
                    F[0, rl[zl], :] = vl[zl]

            for yl in range(5):
                rs = [pl.ds(8 * rblk(c, yl, zl), 8) for zl in range(5) for c in range(3)]
                ims = [IM[pl.ds(8 * (yl * 5 + zl), 8), :] for zl in range(5)]
                news = []
                for i, r in enumerate(rs):
                    now_u = S[cur, r, :]
                    news.append((now_u + now_u) - S[new, r, :] - ims[i // 3] * F[0, r, :])
                for r, v in zip(rs, news):
                    S[new, r, :] = v

            @pl.when(it == STEPS)
            def _():
                @pl.when(me + 2 < nd)
                def _():
                    pl.semaphore_wait(far.at[0], 1)

                @pl.when(me - 2 >= 0)
                def _():
                    pl.semaphore_wait(far.at[1], 1)

                send_patches()
                from_elements(1 - STEPS % 2, 1)

            def add_side(side, first):
                plane = 0 if first == 0 else 1
                rs = [pl.ds(64 * g + first, 8, stride=8) for g in range(ROWS // 8)]
                ds = [pl.ds(8 * g, 8) for g in range(ROWS // 8)]
                news = [
                    S[new, r, :] - IMP[plane, d, :] * recv_dom[side, step, d, :]
                    for r, d in zip(rs, ds)
                ]
                for r, v in zip(rs, news):
                    S[new, r, :] = v

            def left_side():
                @pl.when(step > 0)
                def _():
                    dom_copy(1, step).wait_recv()

                add_side(1, 0)

            @pl.when(jnp.logical_and(has_l, odd))
            def _():
                left_side()

            @pl.when(jnp.logical_and(has_r, step < STEPS - 1))
            def _():
                dom_copy(0, step).wait_recv()
                add_side(0, 4)

            @pl.when(jnp.logical_and(has_l, jnp.logical_not(odd)))
            def _():
                left_side()

        return carry

    lax.fori_loop(0, STEPS + 1, turn, 0)

    from_elements(STEPS % 2, 0)
    for i, off in enumerate(OFFSETS):

        @pl.when(inside(me - off))
        def _(i=i):
            patch_copy(i).wait_recv()
            out_patch[0] = out_patch[0] + precv[i, pl.ds(0, 2), :]

    @pl.when(has_l)
    def _():
        for cp in to_left:
            cp.wait_send()
        for s in range(STEPS - 1):
            dom_copy(0, s).wait_send()

    @pl.when(has_r)
    def _():
        for cp in to_right:
            cp.wait_send()
        for s in range(1, STEPS):
            dom_copy(1, s).wait_send()

    for cp in to_up:
        cp.wait_send()
    for s in range(STEPS):
        dep_copy(0, s).wait_send()
        dep_copy(1, s).wait_send()
    for i, off in enumerate(OFFSETS):

        @pl.when(inside(me + off))
        def _(i=i):
            patch_copy(i).wait_send()


def store_results(cur, fol, patch, out_cur, out_fol, out_patch, sem):
    pairs = ((cur, out_cur), (fol, out_fol), (patch, out_patch))
    copies = [pltpu.make_async_copy(a, b, sem.at[i]) for i, (a, b) in enumerate(pairs)]
    for cp in copies:
        cp.start()
    for cp in copies:
        cp.wait()


def solution(mesh):
    nd, ndp = mesh.shape["dom"], mesh.shape["depth"]

    def on_device(now, nxt, lam, mu, dens, flags, slope, ns, owner):
        any_ = pl.BlockSpec(memory_space=pl.ANY)
        dma = pltpu.SemaphoreType.DMA
        vm = pltpu.VMEM
        i32 = jnp.int32
        cur, fol, patch = pl.pallas_call(
            functools.partial(kernel, nd, ndp),
            name="rupture",
            out_shape=(
                vm((3, 17, 4, 128), f32),
                vm((3, 17, 4, 128), f32),
                vm((1, 2, 128), f32),
            ),
            in_specs=[any_] * 9,
            out_specs=[pl.BlockSpec(memory_space=pltpu.VMEM)] * 3,
            scratch_shapes=[
                vm((2, 3, 17, 8, 128), f32),
                vm((3, 17, 8, 128), f32),
                vm((17, 8, 128), f32),
                vm((2, 2, 1, 4, 32), f32),
                vm((4, 1, 4, 128), i32),
                vm((1, 4, 128), f32),
                vm((1, 4, 128), f32),
                pltpu.SMEM((1, 4), i32),
                vm((3, 4, 1, 4, 128), i32),
                vm((3, 1, 4, 128), f32),
                vm((3, 24, 128), f32),
                vm((3, 24, 128), f32),
                vm((1, 24, 128), f32),
                vm((3, 4, 24, 128), f32),
                vm((25 * 8, 128), f32),
                vm((3, ROWS * 8, 128), f32),
                vm((2, ROWS * 8, 128), f32),
                vm((ROWS * 8, 128), f32),
                vm((ROWS * 8, 128), f32),
                vm((ROWS * 8, 128), f32),
                vm((25 * 8, 128), f32),
                vm((2, ROWS, 128), f32),
                vm((34, 8, 128), f32),
                vm((3, STEPS, 8, 128), f32),
                vm((8, 128), f32),
                vm((2, STEPS, ROWS, 128), f32),
                vm((2, STEPS, ROWS, 128), f32),
                vm((2, STEPS, 3, 8, 128), f32),
                vm((2, STEPS, 3, 8, 128), f32),
                vm((4, 8, 128), f32),
                vm((4, 8, 128), f32),
                dma((10,)),
                dma((12,)),
                dma((12,)),
                dma((2, STEPS)),
                dma((2, STEPS)),
                dma((2, STEPS)),
                dma((2, STEPS)),
                dma((4,)),
                dma((4,)),
                pltpu.SemaphoreType.REGULAR((2,)),
            ],
            compiler_params=pltpu.CompilerParams(collective_id=0, has_side_effects=True),
        )(
            jnp.transpose(now, (0, 2, 1, 3)),
            jnp.transpose(nxt, (0, 2, 1, 3)),
            lam,
            mu,
            jnp.transpose(dens, (1, 0, 2)),
            flags,
            slope,
            ns,
            owner,
        )
        cur, fol, patch = pl.pallas_call(
            store_results,
            name="store_results",
            out_shape=(
                jax.ShapeDtypeStruct((3, 17, 4, 128), f32),
                jax.ShapeDtypeStruct((3, 17, 4, 128), f32),
                jax.ShapeDtypeStruct((1, 2, 128), f32),
            ),
            in_specs=[pl.BlockSpec(memory_space=pltpu.VMEM)] * 3,
            out_specs=[any_] * 3,
            scratch_shapes=[dma((3,))],
        )(*[pltpu.with_memory_space_constraint(v, pltpu.VMEM) for v in (cur, fol, patch)])
        return jnp.transpose(cur, (0, 2, 1, 3)), jnp.transpose(fol, (0, 2, 1, 3)), patch

    return jax.shard_map(
        on_device,
        mesh=mesh,
        in_specs=(
            P(None, "dom", "depth", None),
            P(None, "dom", "depth", None),
            P("dom", "depth", None),
            P("dom", "depth", None),
            P("dom", "depth", None),
            P(None, "depth", "dom", None),
            P("depth", "dom", None),
            P("depth", "dom", None),
            P("depth", "dom"),
        ),
        out_specs=(
            P(None, "dom", "depth", None),
            P(None, "dom", "depth", None),
            P("depth", "dom", None),
        ),
        check_vma=False,
    )
```
